256 devices in a mesh: leaf: 64 (over z, x, core), group: 4 (over y).
Axes of the slice: x: 4, y: 4, z: 8, core: 2. Of those that a mesh axis runs over, the one named last changes fastest.
Arguments:
- q_two: float32 [524288, 256], P(('group', 'leaf'))
- q_one: float32 [524288, 256], P(('group', 'leaf'))
- sources: float32 [524288, 256], P(('group', 'leaf'))
- coupling_two: float32 [2, 256, 256], replicated, as said below
- coupling_one: float32 [256, 256], replicated, as said below
Outputs:
- panel_one: float32 [524288, 256], P(('group', 'leaf'))
- solution: float32 [524288, 256], P(('group', 'leaf'))
Inputs may be any that keep to these rules, and one draw needn't show every extreme that they name: coupling_two[0], coupling_two[1] and coupling_one are symmetric and positive definite. `coupling_one`: symmetric and positive definite.
All inputs are finite; a program needn't handle non-finite values.
Results may differ from the reference program's by a relative error of at most 0.00019.
Values sent between devices are 32-bit elements; how exact they have to be, the bound alone decides.
A program may use at most 64 MiB of HBM per device.

```python
import math
import jax
import jax.numpy as jnp
from jax import lax

LEAF = 2048
R = 256
POINTS = 524288


def noise_draw(key):
    return jax.random.normal(key, (POINTS, R), jnp.float32)


def panel_parts(key):
    base_key = jax.random.fold_in(key, 7301)
    keys = jax.random.split(base_key, 6)
    first = noise_draw(keys[0])
    first = first + 0.6 * jnp.roll(first, 1, axis=1)
    second = noise_draw(keys[1])
    second = second + 0.6 * jnp.roll(second, 1, axis=1)
    third = noise_draw(keys[2])
    unit_two = first
    unit_one = 0.8 * first + 0.6 * second
    unit_src = 0.6 * unit_two + 0.4 * unit_one + 0.7 * third
    positions = jnp.arange(POINTS)
    per_quarter = POINTS // 4 // LEAF
    leaf_pos = (positions // LEAF % per_quarter).astype(jnp.float32)
    rising = jnp.exp(math.log(3.0) * leaf_pos / max(per_quarter - 1, 1))
    rough = jnp.exp(jax.random.uniform(keys[3], (POINTS,), jnp.float32, 0.0, math.log(3.3)))
    row_scale = (rising * rough)[:, None]
    col_two = jnp.exp(jax.random.uniform(keys[4], (R,), jnp.float32, 0.0, math.log(3.0)))[None, :]
    col_one = jnp.exp(jax.random.uniform(keys[5], (R,), jnp.float32, 0.0, math.log(3.0)))[None, :]
    unit = 1.0 / math.sqrt(POINTS / 2 * 17.0)
    panel_two = unit_two * row_scale * col_two * unit
    panel_one = unit_one * row_scale * col_one * unit
    fields = unit_src * row_scale / 3.0
    return (panel_two, panel_one, fields)


def definite_draw(key, count):
    keys = jax.random.split(key, 2)
    values = jax.random.uniform(keys[0], (count, R, R), jnp.float32, -1.0, 1.0)
    upper = jnp.triu(values, 1)
    off_diag = (upper + jnp.swapaxes(upper, 1, 2)) / R
    diag_vals = 1.05 + jnp.exp(jax.random.uniform(keys[1], (count, R), jnp.float32, math.log(0.2), math.log(2.0)))
    return off_diag + jnp.eye(R, dtype=jnp.float32)[None, :, :] * diag_vals[:, :, None]


def draw_q_two(key, part):
    return panel_parts(key)[0]


def draw_q_one(key, part):
    return panel_parts(key)[1]


def draw_sources(key, part):
    return panel_parts(key)[2]


def draw_coupling_two(key, part):
    return definite_draw(jax.random.fold_in(key, 501), 2)


def draw_coupling_one(key, part):
    return definite_draw(jax.random.fold_in(key, 502), 1)[0]


def setup_inputs(seed: int = 0) -> dict:
    arg_keys = jax.random.split(jax.random.key(seed), 6)
    return {
        "q_two": draw_q_two(jax.random.fold_in(arg_keys[5], 71), 0),
        "q_one": draw_q_one(jax.random.fold_in(arg_keys[5], 71), 0),
        "sources": draw_sources(jax.random.fold_in(arg_keys[5], 71), 0),
        "coupling_two": draw_coupling_two(jax.random.fold_in(arg_keys[5], 71), 0),
        "coupling_one": draw_coupling_one(jax.random.fold_in(arg_keys[5], 71), 0),
    }


HIGH = lax.Precision.HIGHEST

def gram_of(left, right):
    return lax.dot_general(left.astype(jnp.float32), right.astype(jnp.float32), (((0,), (0,)), ((), ())), precision=HIGH, preferred_element_type=jnp.float32)

def times_matrix(left, right):
    return jnp.dot(left.astype(jnp.float32), right.astype(jnp.float32), precision=HIGH, preferred_element_type=jnp.float32)

def definite_solve(matrix, target):
    factor = jnp.linalg.cholesky(matrix)
    lower_part = lax.linalg.triangular_solve(factor, target, left_side=True, lower=True)
    return lax.linalg.triangular_solve(factor, lower_part, left_side=True, lower=True, transpose_a=True)

def reference(q_two, q_one, sources, coupling_two, coupling_one):
    half_rows = POINTS // 2
    panels = []
    fields = []
    for which in range(2):
        block_two = q_two[which * half_rows:(which + 1) * half_rows]
        block_one = q_one[which * half_rows:(which + 1) * half_rows]
        block_src = sources[which * half_rows:(which + 1) * half_rows]
        gram_two = gram_of(block_two, block_two)
        cross = gram_of(block_two, block_one)
        projected = gram_of(block_two, block_src)
        solved = definite_solve(coupling_two[which] + gram_two, jnp.concatenate([cross, projected], axis=1))
        update = times_matrix(block_two, solved)
        panels.append(block_one - update[:, :R])
        fields.append(block_src - update[:, R:])
    panel_one = jnp.concatenate(panels, axis=0)
    level_field = jnp.concatenate(fields, axis=0)
    gram_one = gram_of(q_one, panel_one)
    proj_one = gram_of(q_one, level_field)
    weights = definite_solve(coupling_one + gram_one, proj_one)
    solution = level_field - times_matrix(panel_one, weights)
    return (panel_one, solution)
```

```python
import functools
import jax
import jax.numpy as jnp
from jax import lax
from jax.experimental import pallas as pl
from jax.experimental.pallas import tpu as pltpu
from jax.sharding import PartitionSpec as P

HIGH = lax.Precision.HIGHEST
F32 = jnp.float32
B = 16
N = 256
HALF = 128
NC, NX, NZ, NY = 2, 4, 8, 4
PAIRED = 3
STREAMS = 5


def split(value):
    top = value.astype(jnp.bfloat16)
    rest = (value - top.astype(F32)).astype(jnp.bfloat16)
    return top, rest


def dot3(left, right):
    out = jnp.dot(left[0], right[1], preferred_element_type=F32)
    out = out + jnp.dot(left[1], right[0], preferred_element_type=F32)
    return out + jnp.dot(left[0], right[0], preferred_element_type=F32)


def dot3t(left, right):
    dims = (((0,), (0,)), ((), ()))
    out = lax.dot_general(left[0], right[1], dims, preferred_element_type=F32)
    out = out + lax.dot_general(left[1], right[0], dims, preferred_element_type=F32)
    return out + lax.dot_general(left[0], right[0], dims, preferred_element_type=F32)


def gram_kernel(two_ref, one_ref, src_ref, out_ref):
    step = pl.program_id(0)
    two, one, src = split(two_ref[...]), split(one_ref[...]), split(src_ref[...])
    right = [two, one, src]
    for pos, (left, item) in enumerate([(two, two), (two, one), (two, src), (one, one), (one, src)]):
        block = dot3t(left, item)
        for side in range(2):
            part = block[:, side * HALF : (side + 1) * HALF]
            spot = pl.ds(side * N, N)

            @pl.when(step == 0)
            def _():
                out_ref[pos, spot, :] = part

            @pl.when(step > 0)
            def _():
                out_ref[pos, spot, :] += part


def gram_call(q_two, q_one, sources, tile):
    rows = q_two.shape[0]
    spec = pl.BlockSpec((tile, N), lambda i: (i, 0))
    return pl.pallas_call(
        gram_kernel,
        grid=(rows // tile,),
        in_specs=[spec, spec, spec],
        out_specs=pl.BlockSpec((STREAMS, 2 * N, HALF), lambda i: (0, 0, 0)),
        out_shape=jax.ShapeDtypeStruct((STREAMS, 2 * N, HALF), F32),
    )(q_two, q_one, sources)


def here():
    leaf = lax.axis_index("leaf")
    return leaf % NC, (leaf // NC) % NX, leaf // (NC * NX), lax.axis_index("group")


def place(core, x, z, y):
    return {"leaf": (z * NX + x) * NC + core, "group": y}


def neighbours():
    core, x, z, y = here()
    found = [place(1 - core, x, z, y)]
    found += [place(core, (x + d) % NX, z, y) for d in range(1, NX)]
    found += [place(core, x, (z + d) % NZ, y) for d in range(1, NZ)]
    found += [place(core, x, z, (y + d) % NY) for d in range(1, NY)]
    return found


def greet():
    barrier = pltpu.get_barrier_semaphore()
    peers = neighbours()
    for peer in peers:
        pl.semaphore_signal(barrier, inc=1, device_id=peer, device_id_type=pl.DeviceIdType.MESH)
    pl.semaphore_wait(barrier, len(peers))


def stream(pos, g_ref, out_ref, out_pos, core_buf, x_buf, z_buf, y_buf, a1, a2, a3, send, recv):
    core, x, z, y = here()
    paired = pos < PAIRED
    started = []
    count = [0]

    def copy(src, dst, peer):
        slot = count[0]
        count[0] += 1
        item = pltpu.make_async_remote_copy(
            src_ref=src, dst_ref=dst, send_sem=send.at[pos, slot], recv_sem=recv.at[pos, slot],
            device_id=peer, device_id_type=pl.DeviceIdType.MESH)
        item.start()
        started.append(item)
        return item

    mate = place(1 - core, x, z, y)
    first = copy(g_ref.at[pos, pl.ds((1 - core) * 256, 256), :], core_buf.at[pos], mate)
    yield
    first.wait_recv()
    a1[pos] = g_ref[pos, pl.ds(core * 256, 256), :] + core_buf[pos]
    wave = []
    for d in range(1, NX):
        to = (x + d) % NX
        wave.append(copy(a1.at[pos, pl.ds(to * 64, 64), :], x_buf.at[pos, d - 1], place(core, to, z, y)))
    yield
    for item in wave:
        item.wait_recv()
    a2[pos] = (a1[pos, pl.ds(x * 64, 64), :] + x_buf[pos, 1]) + (x_buf[pos, 0] + x_buf[pos, 2])
    wave = []
    for d in range(1, NZ):
        to = (z + d) % NZ
        wave.append(copy(a2.at[pos, pl.ds(to * 8, 8), :], z_buf.at[pos, d - 1], place(core, x, to, y)))
    yield
    for item in wave:
        item.wait_recv()
    total = a2[pos, pl.ds(z * 8, 8), :]
    for d in range(1, NZ):
        total = total + z_buf[pos, d - 1]
    a3[pos] = total
    wave = []
    for d in range(1, NY):
        to = (y + d) % NY
        wave.append(copy(a3.at[pos], y_buf.at[pos, y], place(core, x, z, to)))
    yield
    for item in wave:
        item.wait_recv()
    parts = []
    for q in range(NY):
        parts.append(jnp.where(y == q, total, y_buf[pos, q]))
    spot = core * 256 + x * 64 + z * 8
    if paired:
        out_ref[out_pos, 0, pl.ds(spot, 8), :] = parts[0] + parts[1]
        out_ref[out_pos, 1, pl.ds(spot, 8), :] = parts[2] + parts[3]
    else:
        out_ref[out_pos, pl.ds(spot, 8), :] = (parts[0] + parts[1]) + (parts[2] + parts[3])

    def window(start, size):
        if paired:
            return out_ref.at[out_pos, :, pl.ds(start, size), :]
        return out_ref.at[out_pos, pl.ds(start, size), :]

    wave = []
    for d in range(1, NZ):
        to = (z + d) % NZ
        wave.append(copy(window(spot, 8), window(spot, 8), place(core, x, to, y)))
    yield
    for item in wave:
        item.wait_recv()
    spot = core * 256 + x * 64
    wave = []
    for d in range(1, NX):
        to = (x + d) % NX
        wave.append(copy(window(spot, 64), window(spot, 64), place(core, to, z, y)))
    yield
    for item in wave:
        item.wait_recv()
    spot = core * 256
    last = copy(window(spot, 256), window(spot, 256), mate)
    yield
    last.wait_recv()
    yield
    for item in started:
        item.wait_send()


COPIES = 1 + (NX - 1) + (NZ - 1) + (NY - 1) + (NZ - 1) + (NX - 1) + 1


def reduce_kernel(g_ref, pair_ref, total_ref, *scratch):
    greet()
    lines = []
    for pos in range(STREAMS):
        out_ref, out_pos = (pair_ref, pos) if pos < PAIRED else (total_ref, pos - PAIRED)
        lines.append(stream(pos, g_ref, out_ref, out_pos, *scratch))
    alive = []
    while lines or alive:
        if lines:
            alive.append(lines.pop(0))
        alive = [item for item in alive if next(item, "end") != "end"]


def reduce_call(g):
    vmem = pl.BlockSpec(memory_space=pltpu.VMEM)
    return pl.pallas_call(
        reduce_kernel,
        in_specs=[vmem],
        out_specs=[vmem, vmem],
        out_shape=[
            jax.ShapeDtypeStruct((PAIRED, 2, 2 * N, HALF), F32),
            jax.ShapeDtypeStruct((STREAMS - PAIRED, 2 * N, HALF), F32),
        ],
        scratch_shapes=[
            pltpu.VMEM((STREAMS, 256, HALF), F32),
            pltpu.VMEM((STREAMS, NX - 1, 64, HALF), F32),
            pltpu.VMEM((STREAMS, NZ - 1, 8, HALF), F32),
            pltpu.VMEM((STREAMS, NY, 8, HALF), F32),
            pltpu.VMEM((STREAMS, 256, HALF), F32),
            pltpu.VMEM((STREAMS, 64, HALF), F32),
            pltpu.VMEM((STREAMS, 8, HALF), F32),
            pltpu.SemaphoreType.DMA((STREAMS, COPIES)),
            pltpu.SemaphoreType.DMA((STREAMS, COPIES)),
        ],
        compiler_params=pltpu.CompilerParams(collective_id=0, has_side_effects=True),
    )(g)


def mm(a, b):
    return jnp.dot(a, b, precision=HIGH, preferred_element_type=F32)

def mmt(a, b):
    return lax.dot_general(a, b, (((0,), (0,)), ((), ())), precision=HIGH, preferred_element_type=F32)

def eliminate(rows, base):
    lane = lax.broadcasted_iota(jnp.int32, (B, 128), 1)
    sub = lax.broadcasted_iota(jnp.int32, (B, 128), 0)
    cols = [jnp.broadcast_to(rows[:, base + j : base + j + 1], (B, 128)) for j in range(B)]
    inside = (lane >= base) & (lane < base + B)
    body = jnp.where(inside, jnp.where(lane - base == sub, 1.0, 0.0), rows)
    for k in range(B):
        here = sub == k
        inv = 1.0 / cols[k][k : k + 1, :]
        col = jnp.where(here, -1.0, cols[k])
        for j in range(k + 1, B):
            t = cols[j][k : k + 1, :] * inv
            cols[j] = jnp.where(here, 0.0, cols[j]) - col * t
        t = body[k : k + 1, :] * inv
        body = jnp.where(here, 0.0, body) - col * t
    return body

def invert(refs):
    lane = lax.broadcasted_iota(jnp.int32, (128, 128), 1)
    sub = lax.broadcasted_iota(jnp.int32, (128, 128), 0)
    nblk = 128 // B
    heads = [r[0:B, :] for r in refs]
    for p in range(nblk):
        base = p * B
        in_lane = (lane >= base) & (lane < base + B)
        in_sub = (sub >= base) & (sub < base + B)
        outs = [eliminate(h, base) for h in heads]
        for m, ref in enumerate(refs):
            a = ref[...]
            r = outs[m]
            if p + 1 < nblk:
                nxt = a[base + B : base + 2 * B, :]
                acc = jnp.where(in_lane[:B], 0.0, nxt)
                for j in range(B):
                    acc = acc - jnp.broadcast_to(nxt[:, base + j : base + j + 1], (B, 128)) * r[j : j + 1, :]
                heads[m] = acc
            left = jnp.where(in_lane, jnp.where(in_sub, jnp.where(lane == sub, -1.0, 0.0), a), 0.0)
            parts = []
            if p > 0:
                parts.append(jnp.zeros((base, 128), F32))
            parts.append(r)
            if p + 1 < nblk:
                parts.append(jnp.zeros((128 - base - B, 128), F32))
            right = jnp.concatenate(parts, axis=0) if len(parts) > 1 else r
            ref[...] = jnp.where(in_lane | in_sub, 0.0, a) - mm(left, right)

def solve_all(k_list, z_list, work):
    n = len(k_list)
    for i in range(n):
        work[i][...] = k_list[i][0:128, 0:128]
    invert(work[:n])
    t, zt, z2 = [], [], []
    for i in range(n):
        i1 = work[i][...]
        k12 = k_list[i][0:128, 128:256]
        tk = mm(i1, k12)
        tz = mm(i1, z_list[i][0:128, :])
        z2.append(z_list[i][128:256, :] - mmt(k12, tz))
        t.append(tk); zt.append(tz)
        work[i][...] = k_list[i][128:256, 128:256] - mmt(k12, tk)
    invert(work[:n])
    out = []
    for i in range(n):
        s2 = mm(work[i][...], z2[i])
        s1 = zt[i] - mm(t[i], s2)
        out.append(jnp.concatenate([s1, s2], axis=0))
    return out


def whole(ref, *lead):
    return jnp.concatenate([ref[(*lead, slice(0, N))], ref[(*lead, slice(N, 2 * N))]], axis=1)


def solve_kernel(pair_ref, total_ref, couple_two_ref, couple_one_ref, top_ref, rest_ref, *work):
    half = lax.axis_index("group") // 2
    matrices, targets, crosses = [], [], []
    for h in range(2):
        matrices.append(couple_two_ref[h] + whole(pair_ref, 0, h))
        crosses.append(whole(pair_ref, 1, h))
        targets.append(jnp.concatenate([crosses[h], whole(pair_ref, 2, h)], axis=1))
    solved = solve_all(matrices, targets, work)
    lower = jnp.concatenate([whole(total_ref, 0) + couple_one_ref[...], whole(total_ref, 1)], axis=1)
    for h in range(2):
        lower = lower - mmt(crosses[h], solved[h])
    weights = solve_all([lower[:, :N]], [lower[:, N:]], work)[0]
    mine = jnp.where(half == 0, solved[0], solved[1])
    field = mine[:, N:] - mm(mine[:, :N], weights)
    for pos, item in enumerate([mine[:, :N], field, weights]):
        top, rest = split(item)
        top_ref[:, pos * N : (pos + 1) * N] = top
        rest_ref[:, pos * N : (pos + 1) * N] = rest


def solve_call(pair, total, couple_two, couple_one):
    vmem = pl.BlockSpec(memory_space=pltpu.VMEM)
    shape = jax.ShapeDtypeStruct((N, 3 * N), jnp.bfloat16)
    return pl.pallas_call(
        solve_kernel,
        in_specs=[vmem] * 4,
        out_specs=[vmem, vmem],
        out_shape=[shape, shape],
        scratch_shapes=[pltpu.VMEM((HALF, HALF), F32)] * 2,
    )(pair, total, couple_two, couple_one)


def update_kernel(two_ref, one_ref, src_ref, top_ref, rest_ref, panel_ref, sol_ref):
    two, one = split(two_ref[...]), split(one_ref[...])
    top, rest = top_ref[...], rest_ref[...]
    wide = dot3(two, (top[:, : 2 * N], rest[:, : 2 * N]))
    panel_ref[...] = one_ref[...] - wide[:, :N]
    sol_ref[...] = src_ref[...] - wide[:, N:] - dot3(one, (top[:, 2 * N :], rest[:, 2 * N :]))


def update_call(q_two, q_one, sources, top, rest, tile):
    rows = q_two.shape[0]
    spec = pl.BlockSpec((tile, N), lambda i: (i, 0))
    full = pl.BlockSpec((N, 3 * N), lambda i: (0, 0))
    shape = jax.ShapeDtypeStruct((rows, N), F32)
    return pl.pallas_call(
        update_kernel,
        grid=(rows // tile,),
        in_specs=[spec, spec, spec, full, full],
        out_specs=[spec, spec],
        out_shape=[shape, shape],
    )(q_two, q_one, sources, top, rest)


def per_device(q_two, q_one, sources, coupling_two, coupling_one):
    g = gram_call(q_two, q_one, sources, 512)
    pair, total = reduce_call(g)
    top, rest = solve_call(pair, total, coupling_two, coupling_one)
    panel_one, result = update_call(q_two, q_one, sources, top, rest, 256)
    return (panel_one, result)


def solution(mesh):
    placed = (
        P(("group", "leaf"), None),
        P(("group", "leaf"), None),
        P(("group", "leaf"), None),
        P(),
        P(),
    )
    return jax.shard_map(
        per_device,
        mesh=mesh,
        in_specs=placed,
        out_specs=(P(("group", "leaf"), None), P(("group", "leaf"), None)),
        check_vma=False,
    )
```

```python
import jax
import jax.numpy as jnp
from jax import lax
from jax.experimental import pallas as pl
from jax.experimental.pallas import tpu as pltpu
from jax.sharding import PartitionSpec as P

HIGH = lax.Precision.HIGHEST
F32 = jnp.float32
B = 16
N = 256
HALF = 128
NC, NX, NZ, NY = 2, 4, 8, 4
PAIRED = 3
STREAMS = 5
PHASES = 10
COPIES = 1 + 4 + 2 + (NZ - 1) + (NY - 1) + (NZ - 1) + 2 + 2 + 1


def split(value):
    top = value.astype(jnp.bfloat16)
    rest = (value - top.astype(F32)).astype(jnp.bfloat16)
    return top, rest


def dot3(left, right):
    out = jnp.dot(left[0], right[1], preferred_element_type=F32)
    out = out + jnp.dot(left[1], right[0], preferred_element_type=F32)
    return out + jnp.dot(left[0], right[0], preferred_element_type=F32)


def dot3t(left, right):
    dims = (((0,), (0,)), ((), ()))
    out = lax.dot_general(left[0], right[1], dims, preferred_element_type=F32)
    out = out + lax.dot_general(left[1], right[0], dims, preferred_element_type=F32)
    return out + lax.dot_general(left[0], right[0], dims, preferred_element_type=F32)


def here():
    leaf = lax.axis_index("leaf")
    return leaf % NC, (leaf // NC) % NX, leaf // (NC * NX), lax.axis_index("group")


def place(core, x, z, y):
    return {"leaf": (z * NX + x) * NC + core, "group": y}


def neighbours():
    core, x, z, y = here()
    found = [place(1 - core, x, z, y), place(core, x + 1 - 2 * (x % 2), z, y), place(core, 3 - x, z, y)]
    found += [place(core, x, (z + d) % NZ, y) for d in range(1, NZ)]
    found += [place(core, x, z, (y + d) % NY) for d in range(1, NY)]
    return found


def stream(pos, g_ref, out_ref, out_pos, core_buf, x_buf, mid_buf, last_buf, z_buf, y_buf, a1, a2, a3, send, recv):
    core, x, z, y = here()
    paired = pos < PAIRED
    near, far, across = x + 1 - 2 * (x % 2), 3 - x, (x + 2) % NX
    started = []
    count = [0]

    def copy(src, dst, peer):
        slot = count[0]
        count[0] += 1
        item = pltpu.make_async_remote_copy(
            src_ref=src, dst_ref=dst, send_sem=send.at[pos, slot], recv_sem=recv.at[pos, slot],
            device_id=peer, device_id_type=pl.DeviceIdType.MESH)
        item.start()
        started.append(item)
        return item

    mate = place(1 - core, x, z, y)
    peers = [place(core, near, z, y), place(core, far, z, y)]
    chunks = [near, far]
    first = copy(g_ref.at[pos, pl.ds((1 - core) * 256, 256), :], core_buf.at[pos], mate)
    yield
    first.wait_recv()
    a1[pos] = g_ref[pos, pl.ds(core * 256, 256), :] + core_buf[pos]
    wave = []
    for sub in range(2):
        wave.append(copy(a1.at[pos, pl.ds(across * 64 + sub * 32, 32), :], x_buf.at[pos, sub, 1], peers[sub]))
        wave.append(copy(a1.at[pos, pl.ds(chunks[sub] * 64 + sub * 32, 32), :], x_buf.at[pos, sub, 0], peers[sub]))
    yield
    for item in wave:
        item.wait_recv()
    wave = []
    for sub in range(2):
        mid_buf[pos, sub] = a1[pos, pl.ds(chunks[1 - sub] * 64 + sub * 32, 32), :] + x_buf[pos, sub, 1]
        wave.append(copy(mid_buf.at[pos, sub], last_buf.at[pos, sub], peers[1 - sub]))
    yield
    for sub in range(2):
        wave[sub].wait_recv()
        a2[pos, pl.ds(sub * 32, 32), :] = (
            a1[pos, pl.ds(x * 64 + sub * 32, 32), :] + x_buf[pos, sub, 0] + last_buf[pos, sub])
    wave = []
    for d in range(1, NZ):
        to = (z + d) % NZ
        wave.append(copy(a2.at[pos, pl.ds(to * 8, 8), :], z_buf.at[pos, d - 1], place(core, x, to, y)))
    yield
    for item in wave:
        item.wait_recv()
    total = a2[pos, pl.ds(z * 8, 8), :]
    for d in range(1, NZ):
        total = total + z_buf[pos, d - 1]
    a3[pos] = total
    wave = []
    for d in range(1, NY):
        to = (y + d) % NY
        wave.append(copy(a3.at[pos], y_buf.at[pos, y], place(core, x, z, to)))
    yield
    for item in wave:
        item.wait_recv()
    parts = []
    for q in range(NY):
        parts.append(jnp.where(y == q, a3[pos], y_buf[pos, q]))
    spot = core * 256 + x * 64 + z * 8
    if paired:
        out_ref[out_pos, 0, pl.ds(spot, 8), :] = parts[0] + parts[1]
        out_ref[out_pos, 1, pl.ds(spot, 8), :] = parts[2] + parts[3]
    else:
        out_ref[out_pos, pl.ds(spot, 8), :] = (parts[0] + parts[1]) + (parts[2] + parts[3])

    def window(start, size):
        if paired:
            return out_ref.at[out_pos, :, pl.ds(start, size), :]
        return out_ref.at[out_pos, pl.ds(start, size), :]

    wave = []
    for d in range(1, NZ):
        to = (z + d) % NZ
        wave.append(copy(window(spot, 8), window(spot, 8), place(core, x, to, y)))
    yield
    for item in wave:
        item.wait_recv()
    spot = core * 256 + x * 64
    wave = [copy(window(spot, 64), window(spot, 64), peers[side]) for side in range(2)]
    yield
    for item in wave:
        item.wait_recv()
    wave = []
    for side in range(2):
        spot = core * 256 + chunks[side] * 64 + side * 32
        wave.append(copy(window(spot, 32), window(spot, 32), peers[1 - side]))
    yield
    for item in wave:
        item.wait_recv()
    spot = core * 256
    last = copy(window(spot, 256), window(spot, 256), mate)
    yield
    last.wait_recv()
    yield
    for item in started:
        item.wait_send()


def mm(a, b):
    return jnp.dot(a, b, precision=HIGH, preferred_element_type=F32)

def mmt(a, b):
    return lax.dot_general(a, b, (((0,), (0,)), ((), ())), precision=HIGH, preferred_element_type=F32)

def eliminate(rows, base):
    lane = lax.broadcasted_iota(jnp.int32, (B, 128), 1)
    sub = lax.broadcasted_iota(jnp.int32, (B, 128), 0)
    cols = [jnp.broadcast_to(rows[:, base + j : base + j + 1], (B, 128)) for j in range(B)]
    inside = (lane >= base) & (lane < base + B)
    body = jnp.where(inside, jnp.where(lane - base == sub, 1.0, 0.0), rows)
    for k in range(B):
        here = sub == k
        inv = 1.0 / cols[k][k : k + 1, :]
        col = jnp.where(here, -1.0, cols[k])
        for j in range(k + 1, B):
            t = cols[j][k : k + 1, :] * inv
            cols[j] = jnp.where(here, 0.0, cols[j]) - col * t
        t = body[k : k + 1, :] * inv
        body = jnp.where(here, 0.0, body) - col * t
    return body

def invert(refs):
    lane = lax.broadcasted_iota(jnp.int32, (128, 128), 1)
    sub = lax.broadcasted_iota(jnp.int32, (128, 128), 0)
    nblk = 128 // B
    heads = [r[0:B, :] for r in refs]
    for p in range(nblk):
        base = p * B
        in_lane = (lane >= base) & (lane < base + B)
        in_sub = (sub >= base) & (sub < base + B)
        outs = [eliminate(h, base) for h in heads]
        for m, ref in enumerate(refs):
            a = ref[...]
            r = outs[m]
            if p + 1 < nblk:
                nxt = a[base + B : base + 2 * B, :]
                acc = jnp.where(in_lane[:B], 0.0, nxt)
                for j in range(B):
                    acc = acc - jnp.broadcast_to(nxt[:, base + j : base + j + 1], (B, 128)) * r[j : j + 1, :]
                heads[m] = acc
            left = jnp.where(in_lane, jnp.where(in_sub, jnp.where(lane == sub, -1.0, 0.0), a), 0.0)
            parts = []
            if p > 0:
                parts.append(jnp.zeros((base, 128), F32))
            parts.append(r)
            if p + 1 < nblk:
                parts.append(jnp.zeros((128 - base - B, 128), F32))
            right = jnp.concatenate(parts, axis=0) if len(parts) > 1 else r
            ref[...] = jnp.where(in_lane | in_sub, 0.0, a) - mm(left, right)
        yield


def factor(matrices, work, kept):
    count = len(matrices)
    for i in range(count):
        work[0].at[i][...] = matrices[i][0:HALF, 0:HALF]
    yield from invert([work[0].at[i] for i in range(count)])
    for i in range(count):
        corner = matrices[i][0:HALF, HALF:N]
        kept.append(mm(work[0][i], corner))
        work[1].at[i][...] = matrices[i][HALF:N, HALF:N] - mmt(corner, kept[i])
    yield
    yield from invert([work[1].at[i] for i in range(count)])


def apply(kept, index, target, work):
    upper, lower = target[0:HALF, :], target[HALF:N, :]
    lower = mm(work[1][index], lower - mmt(kept, upper))
    upper = mm(work[0][index], upper) - mm(kept, lower)
    return jnp.concatenate([upper, lower], axis=0)


def whole(ref, *lead):
    return jnp.concatenate([ref[(*lead, slice(0, N))], ref[(*lead, slice(N, 2 * N))]], axis=1)


def main_kernel(two_hbm, one_hbm, src_hbm, couple_two_ref, couple_one_ref, top_ref, rest_ref,
                two_ref, one_ref, src_ref, load_sem, g_ref, pair_ref, total_ref, low, high, *scratch):
    loads = [pltpu.make_async_copy(item, ref, load_sem.at[i]) for i, (item, ref) in
             enumerate([(two_hbm, two_ref), (one_hbm, one_ref), (src_hbm, src_ref)])]
    for item in loads:
        item.start()
    barrier = pltpu.get_barrier_semaphore()
    peers = neighbours()
    for peer in peers:
        pl.semaphore_signal(barrier, inc=1, device_id=peer, device_id_type=pl.DeviceIdType.MESH)
    work = (low, high)

    alive = []

    def tick():
        alive[:] = [item for item in alive if next(item, "end") != "end"]

    def keep(pos, block):
        g_ref[pos, pl.ds(0, N), :] = block[:, :HALF]
        g_ref[pos, pl.ds(N, N), :] = block[:, HALF:]

    def begin(pos):
        out_ref, out_pos = (pair_ref, pos) if pos < PAIRED else (total_ref, pos - PAIRED)
        alive.append(stream(pos, g_ref, out_ref, out_pos, *scratch))
        tick()

    loads[0].wait()
    keep(0, dot3t(split(two_ref[...]), split(two_ref[...])))
    pl.semaphore_wait(barrier, len(peers))
    begin(0)
    loads[1].wait()
    keep(1, dot3t(split(two_ref[...]), split(one_ref[...])))
    begin(1)
    loads[2].wait()
    keep(2, dot3t(split(two_ref[...]), split(src_ref[...])))
    begin(2)
    keep(3, dot3t(split(one_ref[...]), split(one_ref[...])))
    begin(3)
    keep(4, dot3t(split(one_ref[...]), split(src_ref[...])))
    begin(4)
    for _ in range(PHASES - STREAMS):
        tick()
    matrices = [couple_two_ref[h] + whole(pair_ref, 0, h) for h in range(2)]
    kept, left = [], STREAMS - 1
    for step, _ in enumerate(factor(matrices, work, kept)):
        if left and step % 3 == 2:
            tick()
            left -= 1
    for _ in range(left):
        tick()
    half = lax.axis_index("group") // 2
    crosses, solved = [], []
    for h in range(2):
        crosses.append(whole(pair_ref, 1, h))
        solved.append(apply(kept[h], h, jnp.concatenate([crosses[h], whole(pair_ref, 2, h)], axis=1), work))
    lower = jnp.concatenate([whole(total_ref, 0) + couple_one_ref[...], whole(total_ref, 1)], axis=1)
    for h in range(2):
        lower = lower - mmt(crosses[h], solved[h])
    kept = []
    for _ in factor([lower[:, :N]], work, kept):
        pass
    weights = apply(kept[0], 0, lower[:, N:], work)
    mine = jnp.where(half == 0, solved[0], solved[1])
    field = mine[:, N:] - mm(mine[:, :N], weights)
    for pos, item in enumerate([mine[:, :N], field, weights]):
        top, rest = split(item)
        top_ref[:, pos * N : (pos + 1) * N] = top
        rest_ref[:, pos * N : (pos + 1) * N] = rest
    while alive:
        tick()


def main_call(q_two, q_one, sources, couple_two, couple_one):
    vmem = pl.BlockSpec(memory_space=pltpu.VMEM)
    far = pl.BlockSpec(memory_space=pl.ANY)
    shape = jax.ShapeDtypeStruct((N, 3 * N), jnp.bfloat16)
    rows = q_two.shape[0]
    return pl.pallas_call(
        main_kernel,
        in_specs=[far, far, far, vmem, vmem],
        out_specs=[vmem, vmem],
        out_shape=[shape, shape],
        scratch_shapes=[
            pltpu.VMEM((rows, N), F32),
            pltpu.VMEM((rows, N), F32),
            pltpu.VMEM((rows, N), F32),
            pltpu.SemaphoreType.DMA((3,)),
            pltpu.VMEM((STREAMS, 2 * N, HALF), F32),
            pltpu.VMEM((PAIRED, 2, 2 * N, HALF), F32),
            pltpu.VMEM((STREAMS - PAIRED, 2 * N, HALF), F32),
            pltpu.VMEM((2, HALF, HALF), F32),
            pltpu.VMEM((2, HALF, HALF), F32),
            pltpu.VMEM((STREAMS, 256, HALF), F32),
            pltpu.VMEM((STREAMS, 2, 2, 32, HALF), F32),
            pltpu.VMEM((STREAMS, 2, 32, HALF), F32),
            pltpu.VMEM((STREAMS, 2, 32, HALF), F32),
            pltpu.VMEM((STREAMS, NZ - 1, 8, HALF), F32),
            pltpu.VMEM((STREAMS, NY, 8, HALF), F32),
            pltpu.VMEM((STREAMS, 256, HALF), F32),
            pltpu.VMEM((STREAMS, 64, HALF), F32),
            pltpu.VMEM((STREAMS, 8, HALF), F32),
            pltpu.SemaphoreType.DMA((STREAMS, COPIES)),
            pltpu.SemaphoreType.DMA((STREAMS, COPIES)),
        ],
        compiler_params=pltpu.CompilerParams(collective_id=0, has_side_effects=True),
    )(q_two, q_one, sources, couple_two, couple_one)


def update_kernel(two_ref, one_ref, src_ref, top_ref, rest_ref, panel_ref, sol_ref):
    two, one = split(two_ref[...]), split(one_ref[...])
    top, rest = top_ref[...], rest_ref[...]
    wide = dot3(two, (top[:, : 2 * N], rest[:, : 2 * N]))
    panel_ref[...] = one_ref[...] - wide[:, :N]
    sol_ref[...] = src_ref[...] - wide[:, N:] - dot3(one, (top[:, 2 * N :], rest[:, 2 * N :]))


def update_call(q_two, q_one, sources, top, rest, tile):
    rows = q_two.shape[0]
    spec = pl.BlockSpec((tile, N), lambda i: (i, 0))
    full = pl.BlockSpec((N, 3 * N), lambda i: (0, 0))
    shape = jax.ShapeDtypeStruct((rows, N), F32)
    return pl.pallas_call(
        update_kernel,
        grid=(rows // tile,),
        in_specs=[spec, spec, spec, full, full],
        out_specs=[spec, spec],
        out_shape=[shape, shape],
    )(q_two, q_one, sources, top, rest)


def per_device(q_two, q_one, sources, coupling_two, coupling_one):
    top, rest = main_call(q_two, q_one, sources, coupling_two, coupling_one)
    panel_one, result = update_call(q_two, q_one, sources, top, rest, 256)
    return (panel_one, result)


def solution(mesh):
    placed = (
        P(("group", "leaf"), None),
        P(("group", "leaf"), None),
        P(("group", "leaf"), None),
        P(),
        P(),
    )
    return jax.shard_map(
        per_device,
        mesh=mesh,
        in_specs=placed,
        out_specs=(P(("group", "leaf"), None), P(("group", "leaf"), None)),
        check_vma=False,
    )
```

```python
import jax
import jax.numpy as jnp
from jax import lax
from jax.experimental import pallas as pl
from jax.experimental.pallas import tpu as pltpu
from jax.sharding import PartitionSpec as P

HIGH = lax.Precision.HIGHEST
F32 = jnp.float32
B = 16
N = 256
HALF = 128
NC, NX, NZ, NY = 2, 4, 8, 4
PAIRED = 2
STREAMS = 4
FLATS = ((0, 128), (128, 256))
FLAT_COPIES = 1 + (NZ - 1) + (NX * NY - 1) + (NZ - 1) + 1
COPIES = 1 + 4 + 2 + (NZ - 1) + (NY - 1) + (NZ - 1) + 2 + 2 + 1


def split(value):
    top = value.astype(jnp.bfloat16)
    rest = (value - top.astype(F32)).astype(jnp.bfloat16)
    return top, rest


def dot3(left, right):
    out = jnp.dot(left[0], right[1], preferred_element_type=F32)
    out = out + jnp.dot(left[1], right[0], preferred_element_type=F32)
    return out + jnp.dot(left[0], right[0], preferred_element_type=F32)


def dot3t(left, right):
    dims = (((0,), (0,)), ((), ()))
    out = lax.dot_general(left[0], right[1], dims, preferred_element_type=F32)
    out = out + lax.dot_general(left[1], right[0], dims, preferred_element_type=F32)
    return out + lax.dot_general(left[0], right[0], dims, preferred_element_type=F32)


def here():
    leaf = lax.axis_index("leaf")
    return leaf % NC, (leaf // NC) % NX, leaf // (NC * NX), lax.axis_index("group")


def place(core, x, z, y):
    return {"leaf": (z * NX + x) * NC + core, "group": y}


def neighbours():
    core, x, z, y = here()
    found = [place(1 - core, x, z, y)]
    found += [place(core, x, (z + d) % NZ, y) for d in range(1, NZ)]
    found += [place(core, (x + d % NX) % NX, z, (y + d // NX) % NY) for d in range(1, NX * NY)]
    return found


def flat(pos, g_ref, out_ref, core_buf, z_buf, side_buf, a1, a2, send, recv):
    base, rows = FLATS[pos]
    per_core, per_z = rows // NC, rows // NC // NZ
    core, x, z, y = here()
    started = []
    count = [0]

    def copy(src, dst, peer):
        slot = count[0]
        count[0] += 1
        item = pltpu.make_async_remote_copy(
            src_ref=src, dst_ref=dst, send_sem=send.at[pos, slot], recv_sem=recv.at[pos, slot],
            device_id=peer, device_id_type=pl.DeviceIdType.MESH)
        item.start()
        started.append(item)
        return item

    mate = place(1 - core, x, z, y)
    mine = pl.ds(0, per_core)
    tile = pl.ds(0, per_z)
    first = copy(g_ref.at[pl.ds(base + (1 - core) * per_core, per_core), :], core_buf.at[pos, mine, :], mate)
    yield
    first.wait_recv()
    a1[pos, mine, :] = g_ref[pl.ds(base + core * per_core, per_core), :] + core_buf[pos, mine, :]
    wave = []
    for d in range(1, NZ):
        to = (z + d) % NZ
        wave.append(copy(a1.at[pos, pl.ds(to * per_z, per_z), :], z_buf.at[pos, d - 1, tile, :], place(core, x, to, y)))
    yield
    for item in wave:
        item.wait_recv()
    total = a1[pos, pl.ds(z * per_z, per_z), :]
    for d in range(1, NZ):
        total = total + z_buf[pos, d - 1, tile, :]
    a2[pos, tile, :] = total
    wave = []
    for d in range(1, NX * NY):
        to_x, to_y = (x + d % NX) % NX, (y + d // NX) % NY
        wave.append(copy(a2.at[pos, tile, :], side_buf.at[pos, d, tile, :], place(core, to_x, z, to_y)))
    yield
    for item in wave:
        item.wait_recv()
    sums = []
    for back in range(NY):
        part = None
        for d in range(back * NX, back * NX + NX):
            item = a2[pos, tile, :] if d == 0 else side_buf[pos, d, tile, :]
            part = item if part is None else part + item
        sums.append(part)
    spot = base + core * per_core + z * per_z
    own = sums[0] + jnp.where(y % 2 == 1, sums[1], sums[3])
    other = sums[2] + jnp.where(y % 2 == 1, sums[3], sums[1])
    out_ref[0, pl.ds(spot, per_z), :] = jnp.where(y // 2 == 0, own, other)
    out_ref[1, pl.ds(spot, per_z), :] = jnp.where(y // 2 == 0, other, own)
    wave = []
    for d in range(1, NZ):
        to = (z + d) % NZ
        view = out_ref.at[:, pl.ds(spot, per_z), :]
        wave.append(copy(view, view, place(core, x, to, y)))
    yield
    for item in wave:
        item.wait_recv()
    view = out_ref.at[:, pl.ds(base + core * per_core, per_core), :]
    last = copy(view, view, mate)
    yield
    last.wait_recv()
    yield
    for item in started:
        item.wait_send()


FLAT_LOAD = (("core", 32), ("z", 4), ("xy", 4), ("z", 8), ("core", 64))
WIDE_LOAD = (("core", 128), ("x", 32), ("x", 16), ("z", 4), ("y", 4), ("z", 4), ("x", 32), ("x", 16), ("core", 128))
LINK = {"core": (0.0082, 0.9), "x": (0.0215, 1.7), "z": (0.215, 3.3), "y": (0.06, 2.5), "xy": (0.26, 4.0)}


def plan(tasks, jobs):
    loads = []
    for pos in range(len(FLATS)):
        loads.append([(name, size * (1 + pos)) for name, size in FLAT_LOAD])
    for pos in range(STREAMS):
        scale = [1] * 5 + [2 if pos < PAIRED else 1] * 4
        loads.append([(name, size * k) for (name, size), k in zip(WIDE_LOAD, scale)])
    free, due, phase, order = {}, {}, [0] * len(loads), []
    now, jobs_left = 0.0, jobs
    todo = list(tasks)
    while todo or due or jobs_left:
        ready = [item for item in due if due[item] <= now]
        if ready:
            item = min(ready, key=lambda k: (k > 1, due[k]))
            del due[item]
            order.append(("serve", item))
            now += 0.25
            phase[item] += 1
        elif todo:
            kind, item, cost = todo.pop(0)
            order.append((kind, item))
            now += cost
            if kind != "start":
                continue
            phase[item] = 0
        elif jobs_left and phase[0] == len(loads[0]) and (jobs_left > jobs - 8 or phase[1] == len(loads[1])):
            order.append(("job", 0))
            jobs_left -= 1
            now += 0.45
            continue
        else:
            now = min(due.values())
            continue
        if phase[item] < len(loads[item]):
            name, size = loads[item][phase[item]]
            rate, delay = LINK[name]
            lane = name[0]
            begin = max(now, free.get(lane, 0.0))
            free[lane] = begin + rate * size
            due[item] = free[lane] + delay
    return order


def stream(pos, g_ref, out_ref, out_pos, core_buf, x_buf, mid_buf, last_buf, z_buf, y_buf, a1, a2, a3, send, recv):
    core, x, z, y = here()
    paired = pos < PAIRED
    near, far, across = x + 1 - 2 * (x % 2), 3 - x, (x + 2) % NX
    started = []
    count = [0]

    def copy(src, dst, peer):
        slot = count[0]
        count[0] += 1
        item = pltpu.make_async_remote_copy(
            src_ref=src, dst_ref=dst, send_sem=send.at[pos, slot], recv_sem=recv.at[pos, slot],
            device_id=peer, device_id_type=pl.DeviceIdType.MESH)
        item.start()
        started.append(item)
        return item

    mate = place(1 - core, x, z, y)
    peers = [place(core, near, z, y), place(core, far, z, y)]
    chunks = [near, far]
    first = copy(g_ref.at[pos, pl.ds((1 - core) * 256, 256), :], core_buf.at[pos], mate)
    yield
    first.wait_recv()
    a1[pos] = g_ref[pos, pl.ds(core * 256, 256), :] + core_buf[pos]
    wave = []
    for sub in range(2):
        wave.append(copy(a1.at[pos, pl.ds(across * 64 + sub * 32, 32), :], x_buf.at[pos, sub, 1], peers[sub]))
        wave.append(copy(a1.at[pos, pl.ds(chunks[sub] * 64 + sub * 32, 32), :], x_buf.at[pos, sub, 0], peers[sub]))
    yield
    for item in wave:
        item.wait_recv()
    wave = []
    for sub in range(2):
        mid_buf[pos, sub] = a1[pos, pl.ds(chunks[1 - sub] * 64 + sub * 32, 32), :] + x_buf[pos, sub, 1]
        wave.append(copy(mid_buf.at[pos, sub], last_buf.at[pos, sub], peers[1 - sub]))
    yield
    for sub in range(2):
        wave[sub].wait_recv()
        a2[pos, pl.ds(sub * 32, 32), :] = (
            a1[pos, pl.ds(x * 64 + sub * 32, 32), :] + x_buf[pos, sub, 0] + last_buf[pos, sub])
    wave = []
    for d in range(1, NZ):
        to = (z + d) % NZ
        wave.append(copy(a2.at[pos, pl.ds(to * 8, 8), :], z_buf.at[pos, d - 1], place(core, x, to, y)))
    yield
    for item in wave:
        item.wait_recv()
    total = a2[pos, pl.ds(z * 8, 8), :]
    for d in range(1, NZ):
        total = total + z_buf[pos, d - 1]
    a3[pos] = total
    wave = []
    for d in range(1, NY):
        to = (y + d) % NY
        wave.append(copy(a3.at[pos], y_buf.at[pos, y], place(core, x, z, to)))
    yield
    for item in wave:
        item.wait_recv()
    parts = []
    for q in range(NY):
        parts.append(jnp.where(y == q, a3[pos], y_buf[pos, q]))
    spot = core * 256 + x * 64 + z * 8
    if paired:
        out_ref[out_pos, 0, pl.ds(spot, 8), :] = parts[0] + parts[1]
        out_ref[out_pos, 1, pl.ds(spot, 8), :] = parts[2] + parts[3]
    else:
        out_ref[out_pos, pl.ds(spot, 8), :] = (parts[0] + parts[1]) + (parts[2] + parts[3])

    def window(start, size):
        if paired:
            return out_ref.at[out_pos, :, pl.ds(start, size), :]
        return out_ref.at[out_pos, pl.ds(start, size), :]

    wave = []
    for d in range(1, NZ):
        to = (z + d) % NZ
        wave.append(copy(window(spot, 8), window(spot, 8), place(core, x, to, y)))
    yield
    for item in wave:
        item.wait_recv()
    spot = core * 256 + x * 64
    wave = [copy(window(spot, 64), window(spot, 64), peers[side]) for side in range(2)]
    yield
    for item in wave:
        item.wait_recv()
    wave = []
    for side in range(2):
        spot = core * 256 + chunks[side] * 64 + side * 32
        wave.append(copy(window(spot, 32), window(spot, 32), peers[1 - side]))
    yield
    for item in wave:
        item.wait_recv()
    spot = core * 256
    last = copy(window(spot, 256), window(spot, 256), mate)
    yield
    last.wait_recv()
    yield
    for item in started:
        item.wait_send()


def mm(a, b):
    return jnp.dot(a, b, precision=HIGH, preferred_element_type=F32)

def mmt(a, b):
    return lax.dot_general(a, b, (((0,), (0,)), ((), ())), precision=HIGH, preferred_element_type=F32)

def eliminate(rows, base):
    lane = lax.broadcasted_iota(jnp.int32, (B, 128), 1)
    sub = lax.broadcasted_iota(jnp.int32, (B, 128), 0)
    cols = [jnp.broadcast_to(rows[:, base + j : base + j + 1], (B, 128)) for j in range(B)]
    inside = (lane >= base) & (lane < base + B)
    body = jnp.where(inside, jnp.where(lane - base == sub, 1.0, 0.0), rows)
    for k in range(B):
        here = sub == k
        inv = 1.0 / cols[k][k : k + 1, :]
        col = jnp.where(here, -1.0, cols[k])
        for j in range(k + 1, B):
            t = cols[j][k : k + 1, :] * inv
            cols[j] = jnp.where(here, 0.0, cols[j]) - col * t
        t = body[k : k + 1, :] * inv
        body = jnp.where(here, 0.0, body) - col * t
    return body

def invert(refs):
    lane = lax.broadcasted_iota(jnp.int32, (128, 128), 1)
    sub = lax.broadcasted_iota(jnp.int32, (128, 128), 0)
    nblk = 128 // B
    heads = [r[0:B, :] for r in refs]
    for p in range(nblk):
        base = p * B
        in_lane = (lane >= base) & (lane < base + B)
        in_sub = (sub >= base) & (sub < base + B)
        outs = [eliminate(h, base) for h in heads]
        for m, ref in enumerate(refs):
            a = ref[...]
            r = outs[m]
            if p + 1 < nblk:
                nxt = a[base + B : base + 2 * B, :]
                acc = jnp.where(in_lane[:B], 0.0, nxt)
                for j in range(B):
                    acc = acc - jnp.broadcast_to(nxt[:, base + j : base + j + 1], (B, 128)) * r[j : j + 1, :]
                heads[m] = acc
            left = jnp.where(in_lane, jnp.where(in_sub, jnp.where(lane == sub, -1.0, 0.0), a), 0.0)
            parts = []
            if p > 0:
                parts.append(jnp.zeros((base, 128), F32))
            parts.append(r)
            if p + 1 < nblk:
                parts.append(jnp.zeros((128 - base - B, 128), F32))
            right = jnp.concatenate(parts, axis=0) if len(parts) > 1 else r
            ref[...] = jnp.where(in_lane | in_sub, 0.0, a) - mm(left, right)
        yield


def factor(matrices, work, kept, right):
    count = len(matrices)
    for i in range(count):
        work[0].at[i][...] = matrices[i][0]
    yield from invert([work[0].at[i] for i in range(count)])
    for i in range(count):
        corner = right(i, 0)
        kept.append(mm(work[0][i], corner))
        work[1].at[i][...] = right(i, 1) - mmt(corner, kept[i])
    yield
    yield from invert([work[1].at[i] for i in range(count)])


def apply(kept, index, target, work):
    upper, lower = target[0:HALF, :], target[HALF:N, :]
    lower = mm(work[1][index], lower - mmt(kept, upper))
    upper = mm(work[0][index], upper) - mm(kept, lower)
    return jnp.concatenate([upper, lower], axis=0)


def whole(ref, *lead):
    return jnp.concatenate([ref[(*lead, slice(0, N))], ref[(*lead, slice(N, 2 * N))]], axis=1)


def main_kernel(two_hbm, one_hbm, src_hbm, couple_two_ref, couple_one_ref, top_ref, rest_ref,
                two_ref, one_ref, src_ref, load_sem, k_ref, g_ref, base_ref, pair_ref, total_ref, low, high, *scratch):
    loads = [pltpu.make_async_copy(item, ref, load_sem.at[i]) for i, (item, ref) in
             enumerate([(two_hbm, two_ref), (one_hbm, one_ref), (src_hbm, src_ref)])]
    for item in loads:
        item.start()
    barrier = pltpu.get_barrier_semaphore()
    peers = neighbours()
    for peer in peers:
        pl.semaphore_signal(barrier, inc=1, device_id=peer, device_id_type=pl.DeviceIdType.MESH)
    work = (low, high)
    flats = len(FLATS)
    lines = [flat(pos, k_ref, base_ref, *scratch[:7]) for pos in range(flats)]
    for pos in range(STREAMS):
        out_ref, out_pos = (pair_ref, pos) if pos < PAIRED else (total_ref, pos - PAIRED)
        lines.append(stream(pos, g_ref, out_ref, out_pos, *scratch[7:]))
    factors = [(two_ref, one_ref), (two_ref, src_ref), (one_ref, one_ref), (one_ref, src_ref)]

    def keep(pos, block):
        g_ref[pos, pl.ds(0, N), :] = block[:, :HALF]
        g_ref[pos, pl.ds(N, N), :] = block[:, HALF:]

    loads[0].wait()
    first = dot3t(split(two_ref[...]), split(two_ref[...]))
    k_ref[0:HALF, :] = first[:HALF, :HALF]
    k_ref[HALF : HALF + N, :] = first[:, HALF:]
    pl.semaphore_wait(barrier, len(peers))
    kept, jobs = [], None
    tasks = [("start", 0, 0.1), ("start", 1, 0.1)]
    for pos in range(STREAMS):
        tasks += [("gram", pos, 0.9), ("start", flats + pos, 0.1)]

    def level_two():
        matrices = [[couple_two_ref[h, 0:HALF, 0:HALF] + base_ref[h, 0:HALF, :]] for h in range(2)]
        yield from factor(matrices, work, kept, lambda h, part: couple_two_ref[
            h, part * HALF : (part + 1) * HALF, HALF:N] + base_ref[h, (part + 1) * HALF : (part + 2) * HALF, :])

    jobs = level_two()
    for kind, item in plan(tasks, 17):
        if kind == "gram":
            if item < 2:
                loads[item + 1].wait()
            keep(item, dot3t(split(factors[item][0][...]), split(factors[item][1][...])))
        elif kind == "job":
            next(jobs)
        else:
            next(lines[item])
    for _ in jobs:
        raise RuntimeError("jobs left")
    half = lax.axis_index("group") // 2
    crosses, solved = [], []
    for h in range(2):
        crosses.append(whole(pair_ref, 0, h))
        solved.append(apply(kept[h], h, jnp.concatenate([crosses[h], whole(pair_ref, 1, h)], axis=1), work))
    lower = jnp.concatenate([whole(total_ref, 0) + couple_one_ref[...], whole(total_ref, 1)], axis=1)
    for h in range(2):
        lower = lower - mmt(crosses[h], solved[h])
    kept = []
    for _ in factor([[lower[:HALF, :HALF]]], work, kept,
                    lambda _, part: lower[part * HALF : (part + 1) * HALF, HALF:N]):
        pass
    weights = apply(kept[0], 0, lower[:, N:], work)
    mine = jnp.where(half == 0, solved[0], solved[1])
    field = mine[:, N:] - mm(mine[:, :N], weights)
    for pos, item in enumerate([mine[:, :N], field, weights]):
        top, rest = split(item)
        top_ref[:, pos * N : (pos + 1) * N] = top
        rest_ref[:, pos * N : (pos + 1) * N] = rest
    for item in lines:
        for _ in item:
            raise RuntimeError("stream left")


def main_call(q_two, q_one, sources, couple_two, couple_one):
    vmem = pl.BlockSpec(memory_space=pltpu.VMEM)
    far = pl.BlockSpec(memory_space=pl.ANY)
    shape = jax.ShapeDtypeStruct((N, 3 * N), jnp.bfloat16)
    rows = q_two.shape[0]
    return pl.pallas_call(
        main_kernel,
        in_specs=[far, far, far, vmem, vmem],
        out_specs=[vmem, vmem],
        out_shape=[shape, shape],
        scratch_shapes=[
            pltpu.VMEM((rows, N), F32),
            pltpu.VMEM((rows, N), F32),
            pltpu.VMEM((rows, N), F32),
            pltpu.SemaphoreType.DMA((3,)),
            pltpu.VMEM((HALF + N, HALF), F32),
            pltpu.VMEM((STREAMS, 2 * N, HALF), F32),
            pltpu.VMEM((2, HALF + N, HALF), F32),
            pltpu.VMEM((PAIRED, 2, 2 * N, HALF), F32),
            pltpu.VMEM((STREAMS - PAIRED, 2 * N, HALF), F32),
            pltpu.VMEM((2, HALF, HALF), F32),
            pltpu.VMEM((2, HALF, HALF), F32),
            pltpu.VMEM((2, 128, HALF), F32),
            pltpu.VMEM((2, NZ - 1, 16, HALF), F32),
            pltpu.VMEM((2, NX * NY, 16, HALF), F32),
            pltpu.VMEM((2, 128, HALF), F32),
            pltpu.VMEM((2, 16, HALF), F32),
            pltpu.SemaphoreType.DMA((2, FLAT_COPIES)),
            pltpu.SemaphoreType.DMA((2, FLAT_COPIES)),
            pltpu.VMEM((STREAMS, 256, HALF), F32),
            pltpu.VMEM((STREAMS, 2, 2, 32, HALF), F32),
            pltpu.VMEM((STREAMS, 2, 32, HALF), F32),
            pltpu.VMEM((STREAMS, 2, 32, HALF), F32),
            pltpu.VMEM((STREAMS, NZ - 1, 8, HALF), F32),
            pltpu.VMEM((STREAMS, NY, 8, HALF), F32),
            pltpu.VMEM((STREAMS, 256, HALF), F32),
            pltpu.VMEM((STREAMS, 64, HALF), F32),
            pltpu.VMEM((STREAMS, 8, HALF), F32),
            pltpu.SemaphoreType.DMA((STREAMS, COPIES)),
            pltpu.SemaphoreType.DMA((STREAMS, COPIES)),
        ],
        compiler_params=pltpu.CompilerParams(collective_id=0, has_side_effects=True),
    )(q_two, q_one, sources, couple_two, couple_one)


def update_kernel(two_ref, one_ref, src_ref, top_ref, rest_ref, panel_ref, sol_ref):
    two, one = split(two_ref[...]), split(one_ref[...])
    top, rest = top_ref[...], rest_ref[...]
    wide = dot3(two, (top[:, : 2 * N], rest[:, : 2 * N]))
    panel_ref[...] = one_ref[...] - wide[:, :N]
    sol_ref[...] = src_ref[...] - wide[:, N:] - dot3(one, (top[:, 2 * N :], rest[:, 2 * N :]))


def update_call(q_two, q_one, sources, top, rest, tile):
    rows = q_two.shape[0]
    spec = pl.BlockSpec((tile, N), lambda i: (i, 0))
    full = pl.BlockSpec((N, 3 * N), lambda i: (0, 0))
    shape = jax.ShapeDtypeStruct((rows, N), F32)
    return pl.pallas_call(
        update_kernel,
        grid=(rows // tile,),
        in_specs=[spec, spec, spec, full, full],
        out_specs=[spec, spec],
        out_shape=[shape, shape],
    )(q_two, q_one, sources, top, rest)


def per_device(q_two, q_one, sources, coupling_two, coupling_one):
    top, rest = main_call(q_two, q_one, sources, coupling_two, coupling_one)
    panel_one, result = update_call(q_two, q_one, sources, top, rest, 1024)
    return (panel_one, result)


def solution(mesh):
    placed = (
        P(("group", "leaf"), None),
        P(("group", "leaf"), None),
        P(("group", "leaf"), None),
        P(),
        P(),
    )
    return jax.shard_map(
        per_device,
        mesh=mesh,
        in_specs=placed,
        out_specs=(P(("group", "leaf"), None), P(("group", "leaf"), None)),
        check_vma=False,
    )
```

```python
import jax
import jax.numpy as jnp
from jax import lax
from jax.experimental import pallas as pl
from jax.experimental.pallas import tpu as pltpu
from jax.sharding import PartitionSpec as P

HIGH = lax.Precision.HIGHEST
F32 = jnp.float32
B = 16
N = 256
HALF = 128
NC, NX, NZ, NY = 2, 4, 8, 4
PAIRED = 2
STREAMS = 4
EARLY, JOBS = 17, 20
FLATS = ((0, 128), (128, 256))
FLAT_COPIES = 1 + (NZ - 1) + (NX * NY - 1) + (NZ - 1) + 1
COPIES = 1 + 4 + 2 + (NZ - 1) + (NY - 1) + (NZ - 1) + 2 + 2 + 1


def split(value):
    top = value.astype(jnp.bfloat16)
    rest = (value - top.astype(F32)).astype(jnp.bfloat16)
    return top, rest


def dot3(left, right):
    out = jnp.dot(left[0], right[1], preferred_element_type=F32)
    out = out + jnp.dot(left[1], right[0], preferred_element_type=F32)
    return out + jnp.dot(left[0], right[0], preferred_element_type=F32)


def dot3t(left, right):
    dims = (((0,), (0,)), ((), ()))
    out = lax.dot_general(left[0], right[1], dims, preferred_element_type=F32)
    out = out + lax.dot_general(left[1], right[0], dims, preferred_element_type=F32)
    return out + lax.dot_general(left[0], right[0], dims, preferred_element_type=F32)


def here():
    leaf = lax.axis_index("leaf")
    return leaf % NC, (leaf // NC) % NX, leaf // (NC * NX), lax.axis_index("group")


def place(core, x, z, y):
    return {"leaf": (z * NX + x) * NC + core, "group": y}


def neighbours():
    core, x, z, y = here()
    found = [place(1 - core, x, z, y)]
    found += [place(core, x, (z + d) % NZ, y) for d in range(1, NZ)]
    found += [place(core, (x + d % NX) % NX, z, (y + d // NX) % NY) for d in range(1, NX * NY)]
    return found


def flat(pos, g_ref, out_ref, core_buf, z_buf, side_buf, a1, a2, send, recv):
    base, rows = FLATS[pos]
    per_core, per_z = rows // NC, rows // NC // NZ
    core, x, z, y = here()
    started = []
    count = [0]

    def copy(src, dst, peer):
        slot = count[0]
        count[0] += 1
        item = pltpu.make_async_remote_copy(
            src_ref=src, dst_ref=dst, send_sem=send.at[pos, slot], recv_sem=recv.at[pos, slot],
            device_id=peer, device_id_type=pl.DeviceIdType.MESH)
        item.start()
        started.append(item)
        return item

    mate = place(1 - core, x, z, y)
    mine = pl.ds(0, per_core)
    tile = pl.ds(0, per_z)
    first = copy(g_ref.at[pl.ds(base + (1 - core) * per_core, per_core), :], core_buf.at[pos, mine, :], mate)
    yield
    first.wait_recv()
    a1[pos, mine, :] = g_ref[pl.ds(base + core * per_core, per_core), :] + core_buf[pos, mine, :]
    wave = []
    for d in range(1, NZ):
        to = (z + d) % NZ
        wave.append(copy(a1.at[pos, pl.ds(to * per_z, per_z), :], z_buf.at[pos, d - 1, tile, :], place(core, x, to, y)))
    yield
    for item in wave:
        item.wait_recv()
    total = a1[pos, pl.ds(z * per_z, per_z), :]
    for d in range(1, NZ):
        total = total + z_buf[pos, d - 1, tile, :]
    a2[pos, tile, :] = total
    wave = []
    for d in range(1, NX * NY):
        to_x, to_y = (x + d % NX) % NX, (y + d // NX) % NY
        wave.append(copy(a2.at[pos, tile, :], side_buf.at[pos, d, tile, :], place(core, to_x, z, to_y)))
    yield
    for item in wave:
        item.wait_recv()
    sums = []
    for back in range(NY):
        part = None
        for d in range(back * NX, back * NX + NX):
            item = a2[pos, tile, :] if d == 0 else side_buf[pos, d, tile, :]
            part = item if part is None else part + item
        sums.append(part)
    spot = base + core * per_core + z * per_z
    own = sums[0] + jnp.where(y % 2 == 1, sums[1], sums[3])
    other = sums[2] + jnp.where(y % 2 == 1, sums[3], sums[1])
    out_ref[0, pl.ds(spot, per_z), :] = jnp.where(y // 2 == 0, own, other)
    out_ref[1, pl.ds(spot, per_z), :] = jnp.where(y // 2 == 0, other, own)
    wave = []
    for d in range(1, NZ):
        to = (z + d) % NZ
        view = out_ref.at[:, pl.ds(spot, per_z), :]
        wave.append(copy(view, view, place(core, x, to, y)))
    yield
    for item in wave:
        item.wait_recv()
    view = out_ref.at[:, pl.ds(base + core * per_core, per_core), :]
    last = copy(view, view, mate)
    yield
    last.wait_recv()
    yield
    for item in started:
        item.wait_send()


FLAT_LOAD = (("core", 32), ("z", 4), ("xy", 4), ("z", 8), ("core", 64))
WIDE_LOAD = (("core", 128), ("x", 32), ("x", 16), ("z", 4), ("y", 4), ("z", 4), ("x", 32), ("x", 16), ("core", 128))
LINK = {"core": (0.0082, 0.9), "x": (0.0215, 1.7), "z": (0.215, 3.3), "y": (0.06, 2.5), "xy": (0.26, 4.0)}


def needs(job):
    return (0,) if job < 8 else (0, 1) if job < EARLY else (0, 1, 2, 3)


def plan(tasks, jobs):
    loads = []
    for pos in range(len(FLATS)):
        loads.append([(name, size * (1 + pos)) for name, size in FLAT_LOAD])
    for pos in range(STREAMS):
        scale = [1] * 5 + [2 if pos < PAIRED else 1] * 4
        loads.append([(name, size * k) for (name, size), k in zip(WIDE_LOAD, scale)])
    free, due, phase, order = {}, {}, [0] * len(loads), []
    now, jobs_left = 0.0, jobs
    todo = list(tasks)
    while todo or due or jobs_left:
        ready = [item for item in due if due[item] <= now]
        if ready:
            item = min(ready, key=lambda k: (k > 1, k > 3, due[k]))
            del due[item]
            order.append(("serve", item))
            now += 0.25
            phase[item] += 1
        elif todo:
            kind, item, cost = todo.pop(0)
            order.append((kind, item))
            now += cost
            if kind != "start":
                continue
            phase[item] = 0
        elif jobs_left and all(phase[k] == len(loads[k]) for k in needs(jobs - jobs_left)):
            order.append(("job", 0))
            now += 0.45 if jobs - jobs_left < EARLY else 0.9
            jobs_left -= 1
            continue
        else:
            now = min(due.values())
            continue
        if phase[item] < len(loads[item]):
            name, size = loads[item][phase[item]]
            rate, delay = LINK[name]
            lane = name[0]
            begin = max(now, free.get(lane, 0.0))
            free[lane] = begin + rate * size
            due[item] = free[lane] + delay
    return order


def stream(pos, g_ref, out_ref, out_pos, core_buf, x_buf, mid_buf, last_buf, z_buf, y_buf, a1, a2, a3, send, recv):
    core, x, z, y = here()
    paired = pos < PAIRED
    near, far, across = x + 1 - 2 * (x % 2), 3 - x, (x + 2) % NX
    started = []
    count = [0]

    def copy(src, dst, peer):
        slot = count[0]
        count[0] += 1
        item = pltpu.make_async_remote_copy(
            src_ref=src, dst_ref=dst, send_sem=send.at[pos, slot], recv_sem=recv.at[pos, slot],
            device_id=peer, device_id_type=pl.DeviceIdType.MESH)
        item.start()
        started.append(item)
        return item

    mate = place(1 - core, x, z, y)
    peers = [place(core, near, z, y), place(core, far, z, y)]
    chunks = [near, far]
    first = copy(g_ref.at[pos, pl.ds((1 - core) * 256, 256), :], core_buf.at[pos], mate)
    yield
    first.wait_recv()
    a1[pos] = g_ref[pos, pl.ds(core * 256, 256), :] + core_buf[pos]
    wave = []
    for sub in range(2):
        wave.append(copy(a1.at[pos, pl.ds(across * 64 + sub * 32, 32), :], x_buf.at[pos, sub, 1], peers[sub]))
        wave.append(copy(a1.at[pos, pl.ds(chunks[sub] * 64 + sub * 32, 32), :], x_buf.at[pos, sub, 0], peers[sub]))
    yield
    for item in wave:
        item.wait_recv()
    wave = []
    for sub in range(2):
        mid_buf[pos, sub] = a1[pos, pl.ds(chunks[1 - sub] * 64 + sub * 32, 32), :] + x_buf[pos, sub, 1]
        wave.append(copy(mid_buf.at[pos, sub], last_buf.at[pos, sub], peers[1 - sub]))
    yield
    for sub in range(2):
        wave[sub].wait_recv()
        a2[pos, pl.ds(sub * 32, 32), :] = (
            a1[pos, pl.ds(x * 64 + sub * 32, 32), :] + x_buf[pos, sub, 0] + last_buf[pos, sub])
    wave = []
    for d in range(1, NZ):
        to = (z + d) % NZ
        wave.append(copy(a2.at[pos, pl.ds(to * 8, 8), :], z_buf.at[pos, d - 1], place(core, x, to, y)))
    yield
    for item in wave:
        item.wait_recv()
    total = a2[pos, pl.ds(z * 8, 8), :]
    for d in range(1, NZ):
        total = total + z_buf[pos, d - 1]
    a3[pos] = total
    wave = []
    for d in range(1, NY):
        to = (y + d) % NY
        wave.append(copy(a3.at[pos], y_buf.at[pos, y], place(core, x, z, to)))
    yield
    for item in wave:
        item.wait_recv()
    parts = []
    for q in range(NY):
        parts.append(jnp.where(y == q, a3[pos], y_buf[pos, q]))
    spot = core * 256 + x * 64 + z * 8
    if paired:
        out_ref[out_pos, 0, pl.ds(spot, 8), :] = parts[0] + parts[1]
        out_ref[out_pos, 1, pl.ds(spot, 8), :] = parts[2] + parts[3]
    else:
        out_ref[out_pos, pl.ds(spot, 8), :] = (parts[0] + parts[1]) + (parts[2] + parts[3])

    def window(start, size):
        if paired:
            return out_ref.at[out_pos, :, pl.ds(start, size), :]
        return out_ref.at[out_pos, pl.ds(start, size), :]

    wave = []
    for d in range(1, NZ):
        to = (z + d) % NZ
        wave.append(copy(window(spot, 8), window(spot, 8), place(core, x, to, y)))
    yield
    for item in wave:
        item.wait_recv()
    spot = core * 256 + x * 64
    wave = [copy(window(spot, 64), window(spot, 64), peers[side]) for side in range(2)]
    yield
    for item in wave:
        item.wait_recv()
    wave = []
    for side in range(2):
        spot = core * 256 + chunks[side] * 64 + side * 32
        wave.append(copy(window(spot, 32), window(spot, 32), peers[1 - side]))
    yield
    for item in wave:
        item.wait_recv()
    spot = core * 256
    last = copy(window(spot, 256), window(spot, 256), mate)
    yield
    last.wait_recv()
    yield
    for item in started:
        item.wait_send()


def mm(a, b):
    return jnp.dot(a, b, precision=HIGH, preferred_element_type=F32)

def mmt(a, b):
    return lax.dot_general(a, b, (((0,), (0,)), ((), ())), precision=HIGH, preferred_element_type=F32)

def eliminate(rows, base):
    lane = lax.broadcasted_iota(jnp.int32, (B, 128), 1)
    sub = lax.broadcasted_iota(jnp.int32, (B, 128), 0)
    cols = [jnp.broadcast_to(rows[:, base + j : base + j + 1], (B, 128)) for j in range(B)]
    inside = (lane >= base) & (lane < base + B)
    body = jnp.where(inside, jnp.where(lane - base == sub, 1.0, 0.0), rows)
    for k in range(B):
        here = sub == k
        inv = 1.0 / cols[k][k : k + 1, :]
        col = jnp.where(here, -1.0, cols[k])
        for j in range(k + 1, B):
            t = cols[j][k : k + 1, :] * inv
            cols[j] = jnp.where(here, 0.0, cols[j]) - col * t
        t = body[k : k + 1, :] * inv
        body = jnp.where(here, 0.0, body) - col * t
    return body

def invert(refs):
    lane = lax.broadcasted_iota(jnp.int32, (128, 128), 1)
    sub = lax.broadcasted_iota(jnp.int32, (128, 128), 0)
    nblk = 128 // B
    heads = [r[0:B, :] for r in refs]
    for p in range(nblk):
        base = p * B
        in_lane = (lane >= base) & (lane < base + B)
        in_sub = (sub >= base) & (sub < base + B)
        outs = [eliminate(h, base) for h in heads]
        for m, ref in enumerate(refs):
            a = ref[...]
            r = outs[m]
            if p + 1 < nblk:
                nxt = a[base + B : base + 2 * B, :]
                acc = jnp.where(in_lane[:B], 0.0, nxt)
                for j in range(B):
                    acc = acc - jnp.broadcast_to(nxt[:, base + j : base + j + 1], (B, 128)) * r[j : j + 1, :]
                heads[m] = acc
            left = jnp.where(in_lane, jnp.where(in_sub, jnp.where(lane == sub, -1.0, 0.0), a), 0.0)
            parts = []
            if p > 0:
                parts.append(jnp.zeros((base, 128), F32))
            parts.append(r)
            if p + 1 < nblk:
                parts.append(jnp.zeros((128 - base - B, 128), F32))
            right = jnp.concatenate(parts, axis=0) if len(parts) > 1 else r
            ref[...] = jnp.where(in_lane | in_sub, 0.0, a) - mm(left, right)
        yield


def factor(matrices, work, kept, right):
    count = len(matrices)
    for i in range(count):
        work[0].at[i][...] = matrices[i][0]
    yield from invert([work[0].at[i] for i in range(count)])
    for i in range(count):
        corner = right(i, 0)
        kept.append(mm(work[0][i], corner))
        work[1].at[i][...] = right(i, 1) - mmt(corner, kept[i])
    yield
    yield from invert([work[1].at[i] for i in range(count)])


def apply(kept, index, target, work):
    upper, lower = target[0:HALF, :], target[HALF:N, :]
    lower = mm(work[1][index], lower - mmt(kept, upper))
    upper = mm(work[0][index], upper) - mm(kept, lower)
    return jnp.concatenate([upper, lower], axis=0)


def whole(ref, *lead):
    return jnp.concatenate([ref[(*lead, slice(0, N))], ref[(*lead, slice(N, 2 * N))]], axis=1)


def main_kernel(two_hbm, one_hbm, src_hbm, couple_two_hbm, couple_one_hbm, top_ref, rest_ref,
                two_ref, one_ref, src_ref, couple_two_ref, couple_one_ref, load_sem, k_ref, g_ref, base_ref, pair_ref, total_ref, low, high, *scratch):
    barrier = pltpu.get_barrier_semaphore()
    peers = neighbours()
    piece = two_ref.shape[0] // 4
    firsts = [pltpu.make_async_copy(two_hbm.at[pl.ds(i * piece, piece), :], two_ref.at[pl.ds(i * piece, piece), :],
                                    load_sem.at[i]) for i in range(4)]
    for item in firsts:
        item.start()
    for peer in peers:
        pl.semaphore_signal(barrier, inc=1, device_id=peer, device_id_type=pl.DeviceIdType.MESH)
    loads = [pltpu.make_async_copy(item, ref, load_sem.at[4 + i]) for i, (item, ref) in
             enumerate([(one_hbm, one_ref), (src_hbm, src_ref), (couple_two_hbm, couple_two_ref),
                        (couple_one_hbm, couple_one_ref)])]
    work = (low, high)
    flats = len(FLATS)
    lines = [flat(pos, k_ref, base_ref, *scratch[:7]) for pos in range(flats)]
    for pos in range(STREAMS):
        out_ref, out_pos = (pair_ref, pos) if pos < PAIRED else (total_ref, pos - PAIRED)
        lines.append(stream(pos, g_ref, out_ref, out_pos, *scratch[7:]))
    factors = [(two_ref, one_ref), (two_ref, src_ref), (one_ref, one_ref), (one_ref, src_ref)]

    def keep(pos, block):
        g_ref[pos, pl.ds(0, N), :] = block[:, :HALF]
        g_ref[pos, pl.ds(N, N), :] = block[:, HALF:]

    for item in firsts:
        item.wait()
    for item in loads:
        item.start()
    first = dot3t(split(two_ref[...]), split(two_ref[...]))
    k_ref[0:HALF, :] = first[:HALF, :HALF]
    k_ref[HALF : HALF + N, :] = first[:, HALF:]
    pl.semaphore_wait(barrier, len(peers))
    kept = []
    tasks = [("start", 0, 0.1), ("start", 1, 0.1)]
    for pos in range(STREAMS):
        tasks += [("gram", pos, 0.9), ("start", flats + pos, 0.1)]

    crosses, solved, schur = [], [], []

    def level_two():
        for item in loads[2:]:
            item.wait()
        matrices = [[couple_two_ref[h, 0:HALF, 0:HALF] + base_ref[h, 0:HALF, :]] for h in range(2)]
        yield from factor(matrices, work, kept, lambda h, part: couple_two_ref[
            h, part * HALF : (part + 1) * HALF, HALF:N] + base_ref[h, (part + 1) * HALF : (part + 2) * HALF, :])
        for h in range(2):
            crosses.append(whole(pair_ref, 0, h))
            solved.append(apply(kept[h], h, jnp.concatenate([crosses[h], whole(pair_ref, 1, h)], axis=1), work))
            yield
        schur.append(mmt(crosses[0], solved[0]) + mmt(crosses[1], solved[1]))
        yield

    jobs = level_two()
    for kind, item in plan(tasks, JOBS):
        if kind == "gram":
            if item < 2:
                loads[item].wait()
            keep(item, dot3t(split(factors[item][0][...]), split(factors[item][1][...])))
        elif kind == "job":
            next(jobs)
        else:
            next(lines[item])
    for _ in jobs:
        raise RuntimeError("jobs left")
    half = lax.axis_index("group") // 2
    lower = jnp.concatenate([whole(total_ref, 0) + couple_one_ref[...], whole(total_ref, 1)], axis=1) - schur[0]
    kept = []
    for _ in factor([[lower[:HALF, :HALF]]], work, kept,
                    lambda _, part: lower[part * HALF : (part + 1) * HALF, HALF:N]):
        pass
    weights = apply(kept[0], 0, lower[:, N:], work)
    mine = jnp.where(half == 0, solved[0], solved[1])
    field = mine[:, N:] - mm(mine[:, :N], weights)
    for pos, item in enumerate([mine[:, :N], field, weights]):
        top, rest = split(item)
        top_ref[:, pos * N : (pos + 1) * N] = top
        rest_ref[:, pos * N : (pos + 1) * N] = rest
    for item in lines:
        for _ in item:
            raise RuntimeError("stream left")


def main_call(q_two, q_one, sources, couple_two, couple_one):
    vmem = pl.BlockSpec(memory_space=pltpu.VMEM)
    far = pl.BlockSpec(memory_space=pl.ANY)
    shape = jax.ShapeDtypeStruct((N, 3 * N), jnp.bfloat16)
    rows = q_two.shape[0]
    return pl.pallas_call(
        main_kernel,
        in_specs=[far] * 5,
        out_specs=[vmem, vmem],
        out_shape=[shape, shape],
        scratch_shapes=[
            pltpu.VMEM((rows, N), F32),
            pltpu.VMEM((rows, N), F32),
            pltpu.VMEM((rows, N), F32),
            pltpu.VMEM((2, N, N), F32),
            pltpu.VMEM((N, N), F32),
            pltpu.SemaphoreType.DMA((8,)),
            pltpu.VMEM((HALF + N, HALF), F32),
            pltpu.VMEM((STREAMS, 2 * N, HALF), F32),
            pltpu.VMEM((2, HALF + N, HALF), F32),
            pltpu.VMEM((PAIRED, 2, 2 * N, HALF), F32),
            pltpu.VMEM((STREAMS - PAIRED, 2 * N, HALF), F32),
            pltpu.VMEM((2, HALF, HALF), F32),
            pltpu.VMEM((2, HALF, HALF), F32),
            pltpu.VMEM((2, 128, HALF), F32),
            pltpu.VMEM((2, NZ - 1, 16, HALF), F32),
            pltpu.VMEM((2, NX * NY, 16, HALF), F32),
            pltpu.VMEM((2, 128, HALF), F32),
            pltpu.VMEM((2, 16, HALF), F32),
            pltpu.SemaphoreType.DMA((2, FLAT_COPIES)),
            pltpu.SemaphoreType.DMA((2, FLAT_COPIES)),
            pltpu.VMEM((STREAMS, 256, HALF), F32),
            pltpu.VMEM((STREAMS, 2, 2, 32, HALF), F32),
            pltpu.VMEM((STREAMS, 2, 32, HALF), F32),
            pltpu.VMEM((STREAMS, 2, 32, HALF), F32),
            pltpu.VMEM((STREAMS, NZ - 1, 8, HALF), F32),
            pltpu.VMEM((STREAMS, NY, 8, HALF), F32),
            pltpu.VMEM((STREAMS, 256, HALF), F32),
            pltpu.VMEM((STREAMS, 64, HALF), F32),
            pltpu.VMEM((STREAMS, 8, HALF), F32),
            pltpu.SemaphoreType.DMA((STREAMS, COPIES)),
            pltpu.SemaphoreType.DMA((STREAMS, COPIES)),
        ],
        compiler_params=pltpu.CompilerParams(collective_id=0, has_side_effects=True),
    )(q_two, q_one, sources, couple_two, couple_one)


def update_kernel(two_ref, one_ref, src_ref, top_ref, rest_ref, panel_ref, sol_ref):
    two, one = split(two_ref[...]), split(one_ref[...])
    top, rest = top_ref[...], rest_ref[...]
    wide = dot3(two, (top[:, : 2 * N], rest[:, : 2 * N]))
    panel_ref[...] = one_ref[...] - wide[:, :N]
    sol_ref[...] = src_ref[...] - wide[:, N:] - dot3(one, (top[:, 2 * N :], rest[:, 2 * N :]))


def update_call(q_two, q_one, sources, top, rest, tile):
    rows = q_two.shape[0]
    spec = pl.BlockSpec((tile, N), lambda i: (i, 0))
    full = pl.BlockSpec((N, 3 * N), lambda i: (0, 0))
    shape = jax.ShapeDtypeStruct((rows, N), F32)
    return pl.pallas_call(
        update_kernel,
        grid=(rows // tile,),
        in_specs=[spec, spec, spec, full, full],
        out_specs=[spec, spec],
        out_shape=[shape, shape],
    )(q_two, q_one, sources, top, rest)


def per_device(q_two, q_one, sources, coupling_two, coupling_one):
    top, rest = main_call(q_two, q_one, sources, coupling_two, coupling_one)
    panel_one, result = update_call(q_two, q_one, sources, top, rest, 1024)
    return (panel_one, result)


def solution(mesh):
    placed = (
        P(("group", "leaf"), None),
        P(("group", "leaf"), None),
        P(("group", "leaf"), None),
        P(),
        P(),
    )
    return jax.shard_map(
        per_device,
        mesh=mesh,
        in_specs=placed,
        out_specs=(P(("group", "leaf"), None), P(("group", "leaf"), None)),
        check_vma=False,
    )
```

```python
import jax
import jax.numpy as jnp
from jax import lax
from jax.experimental import pallas as pl
from jax.experimental.pallas import tpu as pltpu
from jax.sharding import PartitionSpec as P

HIGH = lax.Precision.HIGHEST
F32 = jnp.float32
B = 16
N = 256
HALF = 128
NC, NX, NZ, NY = 2, 4, 8, 4
PAIRED = 2
STREAMS = 4
EARLY, JOBS, SIDE = 17, 37, 3
FLATS = ((0, 128), (128, 256))
FLAT_COPIES = 1 + (NZ - 1) + (NX * NY - 1) + (NZ - 1) + 1
COPIES = 1 + 4 + 2 + (NZ - 1) + (NY - 1) + (NZ - 1) + 2 + 2 + 1


def split(value):
    top = value.astype(jnp.bfloat16)
    rest = (value - top.astype(F32)).astype(jnp.bfloat16)
    return top, rest


def dot3(left, right):
    out = jnp.dot(left[0], right[1], preferred_element_type=F32)
    out = out + jnp.dot(left[1], right[0], preferred_element_type=F32)
    return out + jnp.dot(left[0], right[0], preferred_element_type=F32)


def dot3t(left, right):
    dims = (((0,), (0,)), ((), ()))
    out = lax.dot_general(left[0], right[1], dims, preferred_element_type=F32)
    out = out + lax.dot_general(left[1], right[0], dims, preferred_element_type=F32)
    return out + lax.dot_general(left[0], right[0], dims, preferred_element_type=F32)


def here():
    leaf = lax.axis_index("leaf")
    return leaf % NC, (leaf // NC) % NX, leaf // (NC * NX), lax.axis_index("group")


def place(core, x, z, y):
    return {"leaf": (z * NX + x) * NC + core, "group": y}


def neighbours():
    core, x, z, y = here()
    found = [place(1 - core, x, z, y)]
    found += [place(core, x, (z + d) % NZ, y) for d in range(1, NZ)]
    found += [place(core, (x + d % NX) % NX, z, (y + d // NX) % NY) for d in range(1, NX * NY)]
    return found


def flat(pos, g_ref, out_ref, core_buf, z_buf, side_buf, a1, a2, send, recv):
    base, rows = FLATS[pos]
    per_core, per_z = rows // NC, rows // NC // NZ
    core, x, z, y = here()
    started = []
    count = [0]

    def copy(src, dst, peer):
        slot = count[0]
        count[0] += 1
        item = pltpu.make_async_remote_copy(
            src_ref=src, dst_ref=dst, send_sem=send.at[pos, slot], recv_sem=recv.at[pos, slot],
            device_id=peer, device_id_type=pl.DeviceIdType.MESH)
        item.start()
        started.append(item)
        return item

    mate = place(1 - core, x, z, y)
    mine = pl.ds(0, per_core)
    tile = pl.ds(0, per_z)
    first = copy(g_ref.at[pl.ds(base + (1 - core) * per_core, per_core), :], core_buf.at[pos, mine, :], mate)
    yield
    first.wait_recv()
    a1[pos, mine, :] = g_ref[pl.ds(base + core * per_core, per_core), :] + core_buf[pos, mine, :]
    wave = []
    for d in range(1, NZ):
        to = (z + d) % NZ
        wave.append(copy(a1.at[pos, pl.ds(to * per_z, per_z), :], z_buf.at[pos, d - 1, tile, :], place(core, x, to, y)))
    yield
    for item in wave:
        item.wait_recv()
    total = a1[pos, pl.ds(z * per_z, per_z), :]
    for d in range(1, NZ):
        total = total + z_buf[pos, d - 1, tile, :]
    a2[pos, tile, :] = total
    wave = []
    for d in range(1, NX * NY):
        to_x, to_y = (x + d % NX) % NX, (y + d // NX) % NY
        wave.append(copy(a2.at[pos, tile, :], side_buf.at[pos, d, tile, :], place(core, to_x, z, to_y)))
    yield
    for item in wave:
        item.wait_recv()
    sums = []
    for back in range(NY):
        part = None
        for d in range(back * NX, back * NX + NX):
            item = a2[pos, tile, :] if d == 0 else side_buf[pos, d, tile, :]
            part = item if part is None else part + item
        sums.append(part)
    spot = base + core * per_core + z * per_z
    own = sums[0] + jnp.where(y % 2 == 1, sums[1], sums[3])
    other = sums[2] + jnp.where(y % 2 == 1, sums[3], sums[1])
    out_ref[0, pl.ds(spot, per_z), :] = jnp.where(y // 2 == 0, own, other)
    out_ref[1, pl.ds(spot, per_z), :] = jnp.where(y // 2 == 0, other, own)
    wave = []
    for d in range(1, NZ):
        to = (z + d) % NZ
        view = out_ref.at[:, pl.ds(spot, per_z), :]
        wave.append(copy(view, view, place(core, x, to, y)))
    yield
    for item in wave:
        item.wait_recv()
    view = out_ref.at[:, pl.ds(base + core * per_core, per_core), :]
    last = copy(view, view, mate)
    yield
    last.wait_recv()
    yield
    for item in started:
        item.wait_send()


FLAT_LOAD = (("core", 32), ("z", 4), ("xy", 4), ("z", 8), ("core", 64))
WIDE_LOAD = (("core", 128), ("x", 32), ("x", 16), ("z", 4), ("y", 4), ("z", 4), ("x", 32), ("x", 16), ("core", 128))
LINK = {"core": (0.0082, 0.9), "x": (0.0215, 1.7), "z": (0.215, 3.3), "y": (0.06, 2.5), "xy": (0.26, 4.0)}


def needs(job):
    return (0,) if job < 8 else (0, 1) if job < EARLY else (0, 1, 2) if job < EARLY + 2 else (0, 1, 2, 3)


def plan(tasks, jobs, sides):
    loads = []
    for pos in range(len(FLATS)):
        loads.append([(name, size * (1 + pos)) for name, size in FLAT_LOAD])
    for pos in range(STREAMS):
        scale = [1] * 5 + [2 - pos % 2] * 4
        loads.append([(name, size * k) for (name, size), k in zip(WIDE_LOAD, scale)])
    free, due, phase, order = {}, {}, [0] * len(loads), []
    now, jobs_left, side = 0.0, jobs, 0
    todo = list(tasks)
    while todo or due or jobs_left or side < sides:
        ready = [item for item in due if due[item] <= now]
        if ready:
            item = min(ready, key=lambda k: (k > 1, k > 3, due[k]))
            del due[item]
            order.append(("serve", item))
            now += 0.25
            phase[item] += 1
        elif todo:
            kind, item, cost = todo.pop(0)
            order.append((kind, item))
            now += cost
            if kind != "start":
                continue
            phase[item] = 0
        elif jobs_left and all(phase[k] == len(loads[k]) for k in needs(jobs - jobs_left)):
            order.append(("job", 0))
            now += 0.45
            jobs_left -= 1
            continue
        elif side < sides and jobs - jobs_left >= EARLY + 2 and all(
                phase[k] == len(loads[k]) for k in ((4,) if side < 2 else (4, 5))):
            order.append(("side", 0))
            now += 0.6
            side += 1
            continue
        else:
            now = min(due.values())
            continue
        if phase[item] < len(loads[item]):
            name, size = loads[item][phase[item]]
            rate, delay = LINK[name]
            lane = name[0]
            begin = max(now, free.get(lane, 0.0))
            free[lane] = begin + rate * size
            due[item] = free[lane] + delay
    return order


def stream(pos, g_ref, out_ref, out_pos, core_buf, x_buf, mid_buf, last_buf, z_buf, y_buf, a1, a2, a3, send, recv):
    core, x, z, y = here()
    paired = pos % 2 == 0
    near, far, across = x + 1 - 2 * (x % 2), 3 - x, (x + 2) % NX
    started = []
    count = [0]

    def copy(src, dst, peer):
        slot = count[0]
        count[0] += 1
        item = pltpu.make_async_remote_copy(
            src_ref=src, dst_ref=dst, send_sem=send.at[pos, slot], recv_sem=recv.at[pos, slot],
            device_id=peer, device_id_type=pl.DeviceIdType.MESH)
        item.start()
        started.append(item)
        return item

    mate = place(1 - core, x, z, y)
    peers = [place(core, near, z, y), place(core, far, z, y)]
    chunks = [near, far]
    first = copy(g_ref.at[pos, pl.ds((1 - core) * 256, 256), :], core_buf.at[pos], mate)
    yield
    first.wait_recv()
    a1[pos] = g_ref[pos, pl.ds(core * 256, 256), :] + core_buf[pos]
    wave = []
    for sub in range(2):
        wave.append(copy(a1.at[pos, pl.ds(across * 64 + sub * 32, 32), :], x_buf.at[pos, sub, 1], peers[sub]))
        wave.append(copy(a1.at[pos, pl.ds(chunks[sub] * 64 + sub * 32, 32), :], x_buf.at[pos, sub, 0], peers[sub]))
    yield
    for item in wave:
        item.wait_recv()
    wave = []
    for sub in range(2):
        mid_buf[pos, sub] = a1[pos, pl.ds(chunks[1 - sub] * 64 + sub * 32, 32), :] + x_buf[pos, sub, 1]
        wave.append(copy(mid_buf.at[pos, sub], last_buf.at[pos, sub], peers[1 - sub]))
    yield
    for sub in range(2):
        wave[sub].wait_recv()
        a2[pos, pl.ds(sub * 32, 32), :] = (
            a1[pos, pl.ds(x * 64 + sub * 32, 32), :] + x_buf[pos, sub, 0] + last_buf[pos, sub])
    wave = []
    for d in range(1, NZ):
        to = (z + d) % NZ
        wave.append(copy(a2.at[pos, pl.ds(to * 8, 8), :], z_buf.at[pos, d - 1], place(core, x, to, y)))
    yield
    for item in wave:
        item.wait_recv()
    total = a2[pos, pl.ds(z * 8, 8), :]
    for d in range(1, NZ):
        total = total + z_buf[pos, d - 1]
    a3[pos] = total
    wave = []
    for d in range(1, NY):
        to = (y + d) % NY
        wave.append(copy(a3.at[pos], y_buf.at[pos, y], place(core, x, z, to)))
    yield
    for item in wave:
        item.wait_recv()
    parts = []
    for q in range(NY):
        parts.append(jnp.where(y == q, a3[pos], y_buf[pos, q]))
    spot = core * 256 + x * 64 + z * 8
    if paired:
        out_ref[out_pos, 0, pl.ds(spot, 8), :] = parts[0] + parts[1]
        out_ref[out_pos, 1, pl.ds(spot, 8), :] = parts[2] + parts[3]
    else:
        out_ref[out_pos, pl.ds(spot, 8), :] = (parts[0] + parts[1]) + (parts[2] + parts[3])

    def window(start, size):
        if paired:
            return out_ref.at[out_pos, :, pl.ds(start, size), :]
        return out_ref.at[out_pos, pl.ds(start, size), :]

    wave = []
    for d in range(1, NZ):
        to = (z + d) % NZ
        wave.append(copy(window(spot, 8), window(spot, 8), place(core, x, to, y)))
    yield
    for item in wave:
        item.wait_recv()
    spot = core * 256 + x * 64
    wave = [copy(window(spot, 64), window(spot, 64), peers[side]) for side in range(2)]
    yield
    for item in wave:
        item.wait_recv()
    wave = []
    for side in range(2):
        spot = core * 256 + chunks[side] * 64 + side * 32
        wave.append(copy(window(spot, 32), window(spot, 32), peers[1 - side]))
    yield
    for item in wave:
        item.wait_recv()
    spot = core * 256
    last = copy(window(spot, 256), window(spot, 256), mate)
    yield
    last.wait_recv()
    yield
    for item in started:
        item.wait_send()


def mm(a, b):
    return jnp.dot(a, b, precision=HIGH, preferred_element_type=F32)

def mmt(a, b):
    return lax.dot_general(a, b, (((0,), (0,)), ((), ())), precision=HIGH, preferred_element_type=F32)

def eliminate(rows, base):
    lane = lax.broadcasted_iota(jnp.int32, (B, 128), 1)
    sub = lax.broadcasted_iota(jnp.int32, (B, 128), 0)
    cols = [jnp.broadcast_to(rows[:, base + j : base + j + 1], (B, 128)) for j in range(B)]
    inside = (lane >= base) & (lane < base + B)
    body = jnp.where(inside, jnp.where(lane - base == sub, 1.0, 0.0), rows)
    for k in range(B):
        here = sub == k
        inv = 1.0 / cols[k][k : k + 1, :]
        col = jnp.where(here, -1.0, cols[k])
        for j in range(k + 1, B):
            t = cols[j][k : k + 1, :] * inv
            cols[j] = jnp.where(here, 0.0, cols[j]) - col * t
        t = body[k : k + 1, :] * inv
        body = jnp.where(here, 0.0, body) - col * t
    return body

def invert(refs):
    lane = lax.broadcasted_iota(jnp.int32, (128, 128), 1)
    sub = lax.broadcasted_iota(jnp.int32, (128, 128), 0)
    nblk = 128 // B
    heads = [r[0:B, :] for r in refs]
    for p in range(nblk):
        base = p * B
        in_lane = (lane >= base) & (lane < base + B)
        in_sub = (sub >= base) & (sub < base + B)
        outs = [eliminate(h, base) for h in heads]
        for m, ref in enumerate(refs):
            a = ref[...]
            r = outs[m]
            if p + 1 < nblk:
                nxt = a[base + B : base + 2 * B, :]
                acc = jnp.where(in_lane[:B], 0.0, nxt)
                for j in range(B):
                    acc = acc - jnp.broadcast_to(nxt[:, base + j : base + j + 1], (B, 128)) * r[j : j + 1, :]
                heads[m] = acc
            left = jnp.where(in_lane, jnp.where(in_sub, jnp.where(lane == sub, -1.0, 0.0), a), 0.0)
            parts = []
            if p > 0:
                parts.append(jnp.zeros((base, 128), F32))
            parts.append(r)
            if p + 1 < nblk:
                parts.append(jnp.zeros((128 - base - B, 128), F32))
            right = jnp.concatenate(parts, axis=0) if len(parts) > 1 else r
            ref[...] = jnp.where(in_lane | in_sub, 0.0, a) - mm(left, right)
        yield


def factor(matrices, work, kept, right):
    count = len(matrices)
    for i in range(count):
        work[0].at[i][...] = matrices[i][0]
    yield from invert([work[0].at[i] for i in range(count)])
    for i in range(count):
        corner = right(i, 0)
        kept.append(mm(work[0][i], corner))
        work[1].at[i][...] = right(i, 1) - mmt(corner, kept[i])
    yield
    yield from invert([work[1].at[i] for i in range(count)])


def apply(kept, index, target, work):
    upper, lower = target[0:HALF, :], target[HALF:N, :]
    parts, head = split(kept), split(upper)
    lower = dot3(split(work[1][index]), split(lower - dot3t(parts, head)))
    upper = dot3(split(work[0][index]), head) - dot3(parts, split(lower))
    return jnp.concatenate([upper, lower], axis=0)


def whole(ref, *lead):
    return jnp.concatenate([ref[(*lead, slice(0, N))], ref[(*lead, slice(N, 2 * N))]], axis=1)


def main_kernel(two_hbm, one_hbm, src_hbm, couple_two_hbm, couple_one_hbm, top_ref, rest_ref,
                two_ref, one_ref, src_ref, couple_two_ref, couple_one_ref, load_sem, k_ref, g_ref, base_ref, pair_ref, total_ref, low, high, *scratch):
    barrier = pltpu.get_barrier_semaphore()
    peers = neighbours()
    piece = two_ref.shape[0] // 4
    firsts = [pltpu.make_async_copy(two_hbm.at[pl.ds(i * piece, piece), :], two_ref.at[pl.ds(i * piece, piece), :],
                                    load_sem.at[i]) for i in range(4)]
    for item in firsts:
        item.start()
    for peer in peers:
        pl.semaphore_signal(barrier, inc=1, device_id=peer, device_id_type=pl.DeviceIdType.MESH)
    loads = [pltpu.make_async_copy(item, ref, load_sem.at[4 + i]) for i, (item, ref) in
             enumerate([(one_hbm, one_ref), (src_hbm, src_ref), (couple_two_hbm, couple_two_ref),
                        (couple_one_hbm, couple_one_ref)])]
    work = (low, high)
    flats = len(FLATS)
    lines = [flat(pos, k_ref, base_ref, *scratch[:7]) for pos in range(flats)]
    for pos in range(STREAMS):
        out_ref, out_pos = (pair_ref if pos % 2 == 0 else total_ref, pos // 2)
        lines.append(stream(pos, g_ref, out_ref, out_pos, *scratch[7:]))
    factors = [(two_ref, one_ref), (one_ref, one_ref), (two_ref, src_ref), (one_ref, src_ref)]

    def keep(pos, block):
        g_ref[pos, pl.ds(0, N), :] = block[:, :HALF]
        g_ref[pos, pl.ds(N, N), :] = block[:, HALF:]

    for item in firsts:
        item.wait()
    for item in loads:
        item.start()
    first = dot3t(split(two_ref[...]), split(two_ref[...]))
    k_ref[0:HALF, :] = first[:HALF, :HALF]
    k_ref[HALF : HALF + N, :] = first[:, HALF:]
    pl.semaphore_wait(barrier, len(peers))
    kept = []
    tasks = [("start", 0, 0.1), ("start", 1, 0.1)]
    for pos in range(STREAMS):
        tasks += [("gram", pos, 0.9), ("start", flats + pos, 0.1)]

    crosses, solved, fields, top, targets = [], [], [], [], []
    last = (low.at[pl.ds(2, 1)], high.at[pl.ds(2, 1)])

    def level_two():
        for item in loads[2:]:
            item.wait()
        matrices = [[couple_two_ref[h, 0:HALF, 0:HALF] + base_ref[h, 0:HALF, :]] for h in range(2)]
        yield from factor(matrices, work, kept, lambda h, part: couple_two_ref[
            h, part * HALF : (part + 1) * HALF, HALF:N] + base_ref[h, (part + 1) * HALF : (part + 2) * HALF, :])
        for h in range(2):
            crosses.append(whole(pair_ref, 0, h))
            solved.append(apply(kept[h], h, crosses[h], work))
            yield
        root = whole(total_ref, 0) + couple_one_ref[...]
        for h in range(2):
            root = root - dot3t(split(crosses[h]), split(solved[h]))
        yield
        yield from factor([[root[:HALF, :HALF]]], last, top, lambda _, part: root[
            part * HALF : (part + 1) * HALF, HALF:N])

    def right_side():
        for h in range(2):
            fields.append(apply(kept[h], h, whole(pair_ref, 1, h), work))
            yield
        value = whole(total_ref, 1)
        for h in range(2):
            value = value - dot3t(split(crosses[h]), split(fields[h]))
        targets.append(value)
        yield

    side = right_side()
    jobs = level_two()
    for kind, item in plan(tasks, JOBS, SIDE):
        if kind == "gram":
            if item % 2 == 0:
                loads[item // 2].wait()
            keep(item, dot3t(split(factors[item][0][...]), split(factors[item][1][...])))
        elif kind == "job":
            next(jobs)
        elif kind == "side":
            next(side)
        else:
            next(lines[item])
    for _ in jobs:
        raise RuntimeError("jobs left")
    half = lax.axis_index("group") // 2
    weights = apply(top[0], 0, targets[0], last)
    mine = jnp.where(half == 0, solved[0], solved[1])
    field = jnp.where(half == 0, fields[0], fields[1]) - dot3(split(mine), split(weights))
    for pos, item in enumerate([mine, field, weights]):
        lead, rest = split(item)
        top_ref[:, pos * N : (pos + 1) * N] = lead
        rest_ref[:, pos * N : (pos + 1) * N] = rest
    for item in lines:
        for _ in item:
            raise RuntimeError("stream left")


def main_call(q_two, q_one, sources, couple_two, couple_one):
    vmem = pl.BlockSpec(memory_space=pltpu.VMEM)
    far = pl.BlockSpec(memory_space=pl.ANY)
    shape = jax.ShapeDtypeStruct((N, 3 * N), jnp.bfloat16)
    rows = q_two.shape[0]
    return pl.pallas_call(
        main_kernel,
        in_specs=[far] * 5,
        out_specs=[vmem, vmem],
        out_shape=[shape, shape],
        scratch_shapes=[
            pltpu.VMEM((rows, N), F32),
            pltpu.VMEM((rows, N), F32),
            pltpu.VMEM((rows, N), F32),
            pltpu.VMEM((2, N, N), F32),
            pltpu.VMEM((N, N), F32),
            pltpu.SemaphoreType.DMA((8,)),
            pltpu.VMEM((HALF + N, HALF), F32),
            pltpu.VMEM((STREAMS, 2 * N, HALF), F32),
            pltpu.VMEM((2, HALF + N, HALF), F32),
            pltpu.VMEM((PAIRED, 2, 2 * N, HALF), F32),
            pltpu.VMEM((STREAMS - PAIRED, 2 * N, HALF), F32),
            pltpu.VMEM((3, HALF, HALF), F32),
            pltpu.VMEM((3, HALF, HALF), F32),
            pltpu.VMEM((2, 128, HALF), F32),
            pltpu.VMEM((2, NZ - 1, 16, HALF), F32),
            pltpu.VMEM((2, NX * NY, 16, HALF), F32),
            pltpu.VMEM((2, 128, HALF), F32),
            pltpu.VMEM((2, 16, HALF), F32),
            pltpu.SemaphoreType.DMA((2, FLAT_COPIES)),
            pltpu.SemaphoreType.DMA((2, FLAT_COPIES)),
            pltpu.VMEM((STREAMS, 256, HALF), F32),
            pltpu.VMEM((STREAMS, 2, 2, 32, HALF), F32),
            pltpu.VMEM((STREAMS, 2, 32, HALF), F32),
            pltpu.VMEM((STREAMS, 2, 32, HALF), F32),
            pltpu.VMEM((STREAMS, NZ - 1, 8, HALF), F32),
            pltpu.VMEM((STREAMS, NY, 8, HALF), F32),
            pltpu.VMEM((STREAMS, 256, HALF), F32),
            pltpu.VMEM((STREAMS, 64, HALF), F32),
            pltpu.VMEM((STREAMS, 8, HALF), F32),
            pltpu.SemaphoreType.DMA((STREAMS, COPIES)),
            pltpu.SemaphoreType.DMA((STREAMS, COPIES)),
        ],
        compiler_params=pltpu.CompilerParams(collective_id=0, has_side_effects=True),
    )(q_two, q_one, sources, couple_two, couple_one)


def update_kernel(two_ref, one_ref, src_ref, top_ref, rest_ref, panel_ref, sol_ref):
    two, one = split(two_ref[...]), split(one_ref[...])
    top, rest = top_ref[...], rest_ref[...]
    wide = dot3(two, (top[:, : 2 * N], rest[:, : 2 * N]))
    panel_ref[...] = one_ref[...] - wide[:, :N]
    sol_ref[...] = src_ref[...] - wide[:, N:] - dot3(one, (top[:, 2 * N :], rest[:, 2 * N :]))


def update_call(q_two, q_one, sources, top, rest, tile):
    rows = q_two.shape[0]
    spec = pl.BlockSpec((tile, N), lambda i: (i, 0))
    full = pl.BlockSpec((N, 3 * N), lambda i: (0, 0))
    shape = jax.ShapeDtypeStruct((rows, N), F32)
    return pl.pallas_call(
        update_kernel,
        grid=(rows // tile,),
        in_specs=[spec, spec, spec, full, full],
        out_specs=[spec, spec],
        out_shape=[shape, shape],
    )(q_two, q_one, sources, top, rest)


def per_device(q_two, q_one, sources, coupling_two, coupling_one):
    top, rest = main_call(q_two, q_one, sources, coupling_two, coupling_one)
    panel_one, result = update_call(q_two, q_one, sources, top, rest, 1024)
    return (panel_one, result)


def solution(mesh):
    placed = (
        P(("group", "leaf"), None),
        P(("group", "leaf"), None),
        P(("group", "leaf"), None),
        P(),
        P(),
    )
    return jax.shard_map(
        per_device,
        mesh=mesh,
        in_specs=placed,
        out_specs=(P(("group", "leaf"), None), P(("group", "leaf"), None)),
        check_vma=False,
    )
```
